32 devices in a mesh: gx: 8 (over y, x, core), gy: 4 (over z).
Axes of the slice: x: 2, y: 2, z: 4, core: 2. Of those that a mesh axis runs over, the one named last changes fastest.
Arguments:
- node_features: bfloat16 [16, 8, 64, 512], P('gx', 'gy'), may hold values from -6 to 6
- edge_features: bfloat16 [3, 16, 8, 64, 512], P(None, 'gx', 'gy'), may hold values from -6 to 6
- open_faces: int32 [3, 16, 8, 64], P(None, 'gx', 'gy'), may hold values 0 or 1
- edge_weight: bfloat16 [1536, 512], replicated, may hold values from -0.15625 to 0.15625
- node_weight: bfloat16 [512, 512], replicated, may hold values from -0.25 to 0.25
- cotangent: bfloat16 [16, 8, 64, 512], P('gx', 'gy'), may hold values from -6 to 6
Outputs:
- new_nodes: bfloat16 [16, 8, 64, 512], P('gx', 'gy')
- node_grad: bfloat16 [16, 8, 64, 512], P('gx', 'gy')
- edge_weight_grad: float32 [786432], P(('gx', 'gy'))
- node_weight_grad: float32 [262144], P(('gx', 'gy'))
The draws below stay inside these ranges and needn't reach their ends.
All inputs are finite; a program needn't handle non-finite values. No bound on the sum of `open_faces` on one device may be relied on, other than what follows from the above.
Results may differ from the reference program's by a relative error of at most 0.013.
Values may be sent and summed in bfloat16 or wider, within the bound.
No kernel may reach another device: no remote copies, remote signals or barrier semaphores. Data moves between devices by JAX's collectives and lax.ppermute only.
A program may use at most 64 MiB of HBM per device.

```python
import jax
import jax.numpy as jnp
from jax import lax

H = 512
NZ = 64
NX = 16
NY = 8


def with_ends(result, own_key, least, high):
    spot = [jax.random.randint(jax.random.fold_in(own_key, axis), (), 0, length) for axis, length in enumerate(result.shape)]
    longest = result.shape.index(max(result.shape))
    beside = spot[:longest] + [(spot[longest] + 1) % result.shape[longest]] + spot[longest + 1:]
    return result.at[tuple(spot)].set(least).at[tuple(beside)].set(high)


def spiked(drawn, own_key, source, target, shards_of, factor):
    owner, partner = [(jnp.arange(drawn.shape[position]) // (drawn.shape[position] // shards_of)).reshape([-1 if axis == position else 1 for axis in range(drawn.ndim)]) for position in (source, target)]
    chosen = jax.random.permutation(own_key, shards_of)[partner]
    strong = (owner == chosen) | (owner == (partner + shards_of // 2) % shards_of)
    return jnp.where(strong, factor * drawn, drawn)


def block_scale(key, extent, cuts, smallest, top_value):
    level = 1.0
    for axis_at, shards_of in cuts:
        draws = jax.random.uniform(jax.random.fold_in(jax.random.fold_in(key, 6), axis_at), (shards_of,), jnp.float32, smallest / len(cuts), top_value / len(cuts))
        level = level * jnp.repeat(jnp.exp(draws), extent[axis_at] // shards_of).reshape((-1,) + (1,) * (len(extent) - 1 - axis_at))
    return level


def scatter_about(rng, extent, spread, reach, split=(), dtype=jnp.bfloat16):
    result = jax.random.normal(rng, extent, jnp.float32) * spread
    if len(split) > 0:
        result = block_scale(rng, extent, split, -0.22, 0.18) * result
    return jnp.clip(result, min=-reach, max=reach).astype(dtype)


def heavy_noise(stream_key, extent, width, bound, shards, heavy, kind=jnp.bfloat16):
    entries = width * jax.random.normal(stream_key, extent, jnp.float32)
    if shards:
        entries = entries * block_scale(stream_key, extent, shards, -0.22, 0.18)
    return jnp.clip(spiked(entries, jax.random.fold_in(stream_key, 3), *heavy), -bound, bound).astype(kind)


def setup_inputs(seed: int = 0) -> dict:
    arg_keys = jax.random.split(jax.random.key(seed), 7)
    node_features = heavy_noise(arg_keys[0], (NX, NY, NZ, H), 1.0, 6.0, ((0, 8), (1, 4)), (0, 3, 8, 2.0))
    edge_features = heavy_noise(arg_keys[1], (3, NX, NY, NZ, H), 1.0, 6.0, ((1, 8), (2, 4)), (1, 4, 8, 2.0))
    open_faces = with_ends((jax.random.randint(arg_keys[2], (3, NX, NY, NZ), 0, 4) < 3).astype(jnp.int32), jax.random.fold_in(arg_keys[2], 1), 0, 1)
    edge_weight = scatter_about(arg_keys[3], (3 * H, H), (3 * H) ** -0.5, 0.15625)
    node_weight = scatter_about(arg_keys[4], (H, H), H ** -0.5, 0.25)
    cotangent = scatter_about(arg_keys[5], (NX, NY, NZ, H), 1.0, 6.0, ((0, 8), (1, 4)))
    return dict(node_features=node_features, edge_features=edge_features, open_faces=open_faces, edge_weight=edge_weight, node_weight=node_weight, cotangent=cotangent)


def silu_slope(values):
    sigmoid = jax.nn.sigmoid(values)
    return sigmoid * (1.0 + values * (1.0 - sigmoid))


def from_above(values, axis_dim):
    length = values.shape[axis_dim]
    trimmed = lax.slice_in_dim(values, 1, length, axis=axis_dim)
    padding = [(0, 0)] * values.ndim
    padding[axis_dim] = (0, 1)
    return jnp.pad(trimmed, padding)


def from_below(values, axis_dim):
    length = values.shape[axis_dim]
    trimmed = lax.slice_in_dim(values, 0, length - 1, axis=axis_dim)
    padding = [(0, 0)] * values.ndim
    padding[axis_dim] = (1, 0)
    return jnp.pad(trimmed, padding)


def rows_of(values):
    return values.reshape(-1, values.shape[-1])


def reference(node_features, edge_features, open_faces, edge_weight, node_weight, cotangent):
    features = node_features.shape[-1]
    shape = node_features.shape
    self_weight = edge_weight[:features]
    other_weight = edge_weight[features:2 * features]
    stored_weight = edge_weight[2 * features:]
    summed = jnp.zeros(shape, jnp.float32)
    preacts, neighbours, open_masks = [], [], []
    for direction in range(3):
        neighbour = from_above(node_features, direction)
        length = shape[direction]
        inside = (jnp.arange(length) < length - 1).astype(jnp.float32)
        broadcast_shape = [1, 1, 1]
        broadcast_shape[direction] = length
        open_mask = open_faces[direction].astype(jnp.float32) * inside.reshape(broadcast_shape)
        preact = (jnp.dot(rows_of(node_features), self_weight, preferred_element_type=jnp.float32)
                  + jnp.dot(rows_of(neighbour), other_weight, preferred_element_type=jnp.float32)
                  + jnp.dot(rows_of(edge_features[direction]), stored_weight, preferred_element_type=jnp.float32)).reshape(shape)
        message = (jax.nn.silu(preact) * open_mask[..., None]).astype(jnp.bfloat16)
        widened = message.astype(jnp.float32)
        summed = summed + widened - from_below(widened, direction)
        preacts.append(preact)
        neighbours.append(neighbour)
        open_masks.append(open_mask)
    summed_half = summed.astype(jnp.bfloat16)
    update = jnp.dot(rows_of(summed_half), node_weight, preferred_element_type=jnp.float32).reshape(shape)
    new_nodes = (node_features.astype(jnp.float32) + jax.nn.silu(update)).astype(jnp.bfloat16)
    grad_update = (cotangent.astype(jnp.float32) * silu_slope(update)).astype(jnp.bfloat16)
    node_weight_grad = jnp.dot(rows_of(summed_half).T, rows_of(grad_update), preferred_element_type=jnp.float32)
    grad_summed = jnp.dot(rows_of(grad_update), node_weight.T, preferred_element_type=jnp.float32).reshape(shape).astype(jnp.bfloat16)
    grad_wide = grad_summed.astype(jnp.float32)
    node_grad = cotangent.astype(jnp.float32)
    self_grad = jnp.zeros((features, features), jnp.float32)
    other_grad = jnp.zeros((features, features), jnp.float32)
    stored_grad = jnp.zeros((features, features), jnp.float32)
    for direction in range(3):
        grad_message = grad_wide - from_above(grad_wide, direction)
        grad_preact = (grad_message * open_masks[direction][..., None] * silu_slope(preacts[direction])).astype(jnp.bfloat16)
        flat_grad = rows_of(grad_preact)
        self_grad = self_grad + jnp.dot(rows_of(node_features).T, flat_grad, preferred_element_type=jnp.float32)
        other_grad = other_grad + jnp.dot(rows_of(neighbours[direction]).T, flat_grad, preferred_element_type=jnp.float32)
        stored_grad = stored_grad + jnp.dot(rows_of(edge_features[direction]).T, flat_grad, preferred_element_type=jnp.float32)
        own_term = jnp.dot(flat_grad, self_weight.T, preferred_element_type=jnp.float32).reshape(shape)
        upper_term = jnp.dot(flat_grad, other_weight.T, preferred_element_type=jnp.float32).reshape(shape)
        node_grad = node_grad + own_term + from_below(upper_term, direction)
    edge_weight_grad = jnp.concatenate([self_grad, other_grad, stored_grad], axis=0)
    return new_nodes, node_grad.astype(jnp.bfloat16), edge_weight_grad.reshape(-1), node_weight_grad.reshape(-1)
```

```python
import functools

import jax
import jax.numpy as jnp
from jax import lax
from jax.experimental import pallas as pl
from jax.experimental.pallas import tpu as pltpu
from jax.sharding import PartitionSpec as P

F32 = jnp.float32
BF16 = jnp.bfloat16
PAD = 16


def passed_along(value, axis, steps):
    count = lax.axis_size(axis)
    first, last = (max(0, -steps), min(count, count - steps))
    return lax.ppermute(value, axis, [(source, source + steps) for source in range(first, last)])


def exchanged(value, axis, flip):
    count = lax.axis_size(axis)
    return lax.ppermute(value, axis, [(source, source ^ flip) for source in range(count)])


def dot(left, right):
    return jnp.dot(left, right, preferred_element_type=F32)


def dot_nt(left, right):
    return lax.dot_general(left, right, (((1,), (1,)), ((), ())), preferred_element_type=F32)


def dot_tn(left, right):
    return lax.dot_general(left, right, (((0,), (0,)), ((), ())), preferred_element_type=F32)


def column_of(row):
    size = row.shape[-1]
    spread = jnp.broadcast_to(row, (size, size))
    down = lax.broadcasted_iota(jnp.int32, (size, size), 0)
    across = lax.broadcasted_iota(jnp.int32, (size, size), 1)
    return jnp.sum(jnp.where(down == across, spread, 0.0), axis=1, keepdims=True)


def sigmoid(values):
    return 0.5 * jnp.tanh(0.5 * values) + 0.5


def call(kernel, outs, args, scratch=(), limit=60 << 20, cost=None):
    return pl.pallas_call(
        kernel,
        out_shape=[jax.ShapeDtypeStruct(shape, dtype) for shape, dtype in outs],
        in_specs=[pl.BlockSpec(memory_space=pltpu.VMEM)] * len(args),
        out_specs=[pl.BlockSpec(memory_space=pltpu.VMEM)] * len(outs),
        scratch_shapes=list(scratch),
        compiler_params=pltpu.CompilerParams(vmem_limit_bytes=limit),
        cost_estimate=cost,
    )(*args)


def products_kernel(node_ref, edge_ref, weight_ref, stored_ref, other_ref):
    features = node_ref.shape[-1]
    node = node_ref[...].reshape(-1, features)
    own = dot(node, weight_ref[:features])
    other_ref[...] = dot(node, weight_ref[features : 2 * features])
    for direction in range(3):
        edge = edge_ref[direction].reshape(-1, features)
        stored_ref[direction] = own + dot(edge, weight_ref[2 * features :])


def layer_kernel(
    dims,
    stored_ref, other_ref, weight_ref, node_weight_ref, node_ref, edge_ref, open_ref, cotangent_ref,
    above_first_ref, above_second_ref, below_first_ref, below_second_ref,
    new_ref, low_first_ref, low_second_ref, top_first_ref, top_second_ref,
    own_ref, enter_ref, slope_top_first_ref, slope_top_second_ref, slope_low_first_ref, slope_low_second_ref,
    send_ref, keep_ref,
    summed_ref, update_ref, slope_ref, slope_low_ref, message_ref, message_low_ref,
    grads_ref, total_ref,
):
    ex, ey, nz, features = dims
    at_first, at_second = lax.axis_index("gx"), lax.axis_index("gy")
    inside_first = (at_first < lax.axis_size("gx") - 1).astype(F32)
    inside_second = (at_second < lax.axis_size("gy") - 1).astype(F32)
    self_weight = weight_ref[:features]
    other_weight = weight_ref[features : 2 * features]
    stored_weight = weight_ref[2 * features :]

    def rows(x, y):
        return slice((x * ey + y) * nz, (x * ey + y + 1) * nz)

    def part(index):
        return slice(index * nz, (index + 1) * nz)

    def edge_terms(preact, open_column):
        gate = sigmoid(preact)
        opened = gate * open_column
        message = (preact * opened).astype(BF16).astype(F32)
        return message, opened * (1.0 + preact * (1.0 - gate))

    edge_rows_first, edge_rows_second = ey * nz, ex * nz
    above_first = dot(above_first_ref[...], other_weight)
    above_second = dot(above_second_ref[...], other_weight)
    node_below_first = below_first_ref[:edge_rows_first]
    edge_below_first = below_first_ref[edge_rows_first : 2 * edge_rows_first]
    node_below_second = below_second_ref[:edge_rows_second]
    edge_below_second = below_second_ref[edge_rows_second : 2 * edge_rows_second]
    low_first = dot(node_below_first, self_weight) + dot(edge_below_first, stored_weight)
    low_second = dot(node_below_second, self_weight) + dot(edge_below_second, stored_weight)
    mask_first = below_first_ref[2 * edge_rows_first :].astype(F32)
    mask_second = below_second_ref[2 * edge_rows_second :].astype(F32)
    down = lax.broadcasted_iota(jnp.int32, (nz, 1), 0)
    inside_third = jnp.where(down < nz - 1, 1.0, 0.0)
    opened = open_ref[...].astype(F32)

    for y in range(ey):
        message, slope = edge_terms(low_first[part(y)] + other_ref[rows(0, y)], column_of(mask_first[y : y + 1, :nz]))
        message_low_ref[part(y)] = message
        slope_low_ref[part(y)] = slope
    for x in range(ex):
        at = part(ey + x)
        message, slope = edge_terms(low_second[part(x)] + other_ref[rows(x, 0)], column_of(mask_second[x : x + 1, :nz]))
        message_low_ref[at] = message
        slope_low_ref[at] = slope
    for x in range(ex):
        for y in range(ey):
            here = rows(x, y)
            column = [
                column_of(opened[(direction * ex + x) * ey + y : (direction * ex + x) * ey + y + 1]) for direction in range(3)
            ]
            if x + 1 < ex:
                beyond = other_ref[rows(x + 1, y)]
            else:
                beyond, column[0] = above_first[part(y)], column[0] * inside_first
            message_ref[0, here], slope_ref[0, here] = edge_terms(stored_ref[0, here] + beyond, column[0])
            if y + 1 < ey:
                beyond = other_ref[rows(x, y + 1)]
            else:
                beyond, column[1] = above_second[part(x)], column[1] * inside_second
            message_ref[1, here], slope_ref[1, here] = edge_terms(stored_ref[1, here] + beyond, column[1])
            beyond = pltpu.roll(other_ref[here], nz - 1, 0)
            message_ref[2, here], slope_ref[2, here] = edge_terms(stored_ref[2, here] + beyond, column[2] * inside_third)
    for x in range(ex):
        for y in range(ey):
            here = rows(x, y)
            third = message_ref[2, here]
            total = message_ref[0, here] + message_ref[1, here] + third - pltpu.roll(third, 1, 0)
            total = total - (message_ref[0, rows(x - 1, y)] if x > 0 else message_low_ref[part(y)])
            total = total - (message_ref[1, rows(x, y - 1)] if y > 0 else message_low_ref[part(ey + x)])
            summed_ref[here] = total.astype(BF16)

    node = node_ref[...].reshape(-1, features)
    update = dot(summed_ref[...], node_weight_ref[...])
    gate = sigmoid(update)
    new_ref[...] = (node.astype(F32) + update * gate).astype(BF16).reshape(new_ref.shape)
    cotangent = cotangent_ref[...].reshape(-1, features).astype(F32)
    update_ref[...] = (cotangent * (gate * (1.0 + update * (1.0 - gate)))).astype(BF16)
    grad_summed = dot_nt(update_ref[...], node_weight_ref[...]).astype(BF16)
    for y in range(ey):
        low_first_ref[part(y)] = grad_summed[rows(0, y)]
        top_first_ref[part(y)] = grad_summed[rows(ex - 1, y)]
    for x in range(ex):
        low_second_ref[part(x)] = grad_summed[rows(x, 0)]
        top_second_ref[part(x)] = grad_summed[rows(x, ey - 1)]
    wide = grad_summed.astype(F32)

    count = ex * ey * nz
    for y in range(ey):
        entering = -wide[rows(0, y)] * slope_low_ref[part(y)]
        message_low_ref[part(y)] = entering
        grads_ref[3 * count + y * nz : 3 * count + (y + 1) * nz] = entering.astype(BF16)
    for x in range(ex):
        at = part(ey + x)
        entering = -wide[rows(x, 0)] * slope_low_ref[at]
        message_low_ref[at] = entering
        start = 3 * count + (ey + x) * nz
        grads_ref[start : start + nz] = entering.astype(BF16)
    for x in range(ex):
        for y in range(ey):
            here = rows(x, y)
            mine = wide[here]
            lead = [
                mine - wide[rows(x + 1, y)] if x + 1 < ex else mine,
                mine - wide[rows(x, y + 1)] if y + 1 < ey else mine,
                mine - pltpu.roll(mine, nz - 1, 0),
            ]
            for direction in range(3):
                grad = lead[direction] * slope_ref[direction, here]
                message_ref[direction, here] = grad
                start = direction * count + (x * ey + y) * nz
                grads_ref[start : start + nz] = grad.astype(BF16)
    for x in range(ex):
        for y in range(ey):
            here = rows(x, y)
            third = message_ref[2, here]
            own_ref[here] = message_ref[0, here] + message_ref[1, here] + third
            enter = pltpu.roll(third, 1, 0)
            enter = enter + (message_ref[0, rows(x - 1, y)] if x > 0 else message_low_ref[part(y)])
            enter = enter + (message_ref[1, rows(x, y - 1)] if y > 0 else message_low_ref[part(ey + x)])
            enter_ref[here] = enter
    for y in range(ey):
        slope_top_first_ref[part(y)] = slope_ref[0, rows(ex - 1, y)]
        slope_low_first_ref[part(y)] = slope_low_ref[part(y)]
    for x in range(ex):
        slope_top_second_ref[part(x)] = slope_ref[1, rows(x, ey - 1)]
        slope_low_second_ref[part(x)] = slope_low_ref[part(ey + x)]

    grads_low = grads_ref[3 * count :]
    total_ref[:features] = dot_tn(
        jnp.concatenate([node, node_below_first, node_below_second], axis=0),
        jnp.concatenate([own_ref[...].astype(BF16), grads_low], axis=0),
    )
    tops = [grads_ref[(x * ey + y) * nz : (x * ey + y + 1) * nz] for x in [ex - 1] for y in range(ey)]
    tops += [grads_ref[count + (x * ey + y) * nz : count + (x * ey + y + 1) * nz] for x in range(ex) for y in [ey - 1]]
    total_ref[features : 2 * features] = dot_tn(
        jnp.concatenate([node, above_first_ref[...], above_second_ref[...]], axis=0),
        jnp.concatenate([enter_ref[...].astype(BF16), *tops], axis=0),
    )
    edges = edge_ref[...].reshape(-1, features)
    total_ref[2 * features : 3 * features] = dot_tn(
        jnp.concatenate([edges, edge_below_first, edge_below_second], axis=0), grads_ref[...]
    )
    total_ref[3 * features :] = dot_tn(summed_ref[...], update_ref[...])

    if send_ref is None:
        keep_ref[...] = total_ref[...]
        return
    planes, seconds, chunk = send_ref.shape[0], lax.axis_size("gy"), send_ref.shape[1] // lax.axis_size("gy")
    edge_rows, node_rows = chunk * 3 // 4, chunk // 4
    core, plane = at_first % 2, at_first // 2
    for block in range(planes):
        for second in range(seconds):
            there = (plane ^ block) * 2
            for target, flip in ((keep_ref, core), (send_ref, 1 - core)):
                device = (there + flip) * seconds + (at_second ^ second)
                edge_at = pl.multiple_of(device * edge_rows, 8)
                node_at = pl.multiple_of(3 * features + device * node_rows, 8)
                start = second * chunk
                target[block, start : start + edge_rows] = total_ref[pl.ds(edge_at, edge_rows)].astype(target.dtype)
                target[block, start + edge_rows : start + chunk] = total_ref[pl.ds(node_at, node_rows)].astype(target.dtype)


def node_grad_kernel(
    dims, own_ref, enter_ref, slope_top_first_ref, slope_top_second_ref, slope_low_first_ref, slope_low_second_ref,
    above_first_ref, above_second_ref, below_first_ref, below_second_ref, cotangent_ref, weight_ref, out_ref,
):
    ex, ey, nz, features = dims

    def rows(x, y):
        return slice((x * ey + y) * nz, (x * ey + y + 1) * nz)

    def part(index):
        return slice(index * nz, (index + 1) * nz)

    own, enter = [], []
    for x in range(ex):
        for y in range(ey):
            grad = own_ref[rows(x, y)]
            if x == ex - 1:
                grad = grad - above_first_ref[part(y)].astype(F32) * slope_top_first_ref[part(y)]
            if y == ey - 1:
                grad = grad - above_second_ref[part(x)].astype(F32) * slope_top_second_ref[part(x)]
            own.append(grad.astype(BF16))
            grad = enter_ref[rows(x, y)]
            if x == 0:
                grad = grad + below_first_ref[part(y)].astype(F32) * slope_low_first_ref[part(y)]
            if y == 0:
                grad = grad + below_second_ref[part(x)].astype(F32) * slope_low_second_ref[part(x)]
            enter.append(grad.astype(BF16))
    result = dot_nt(jnp.concatenate(own, axis=0), weight_ref[:features])
    result = result + dot_nt(jnp.concatenate(enter, axis=0), weight_ref[features : 2 * features])
    result = result + cotangent_ref[...].reshape(-1, features).astype(F32)
    out_ref[...] = result.astype(BF16).reshape(out_ref.shape)


def pair_sum_kernel(keep_ref, received_ref, kept_ref, *send_refs):
    kept_ref[...] = keep_ref[0] + received_ref[0].astype(F32)
    for index, send_ref in enumerate(send_refs):
        send_ref[...] = (keep_ref[index + 1] + received_ref[index + 1].astype(F32)).astype(BF16)


def plane_sum_kernel(groups, keep_ref, *refs):
    received, kept_ref, send_refs = refs[: groups[0] - 1], refs[groups[0] - 1], refs[groups[0] :]
    chunk = kept_ref.shape[0]
    for index in range(groups[1]):
        here = slice(index * chunk, (index + 1) * chunk)
        total = keep_ref[here]
        for ref in received:
            total = total + ref[here].astype(F32)
        if index == 0:
            kept_ref[...] = total
        else:
            send_refs[index - 1][...] = total.astype(BF16)


def last_sum_kernel(keep_ref, *refs):
    received, edge_ref, node_ref = refs[:-2], refs[-2], refs[-1]
    total = keep_ref[...]
    for ref in received:
        total = total + ref[...].astype(F32)
    lanes = edge_ref.shape[1]
    pieces = total.shape[1] // lanes
    edge_rows, node_rows = edge_ref.shape[0] // pieces, node_ref.shape[0] // pieces
    for piece in range(pieces):
        across = slice(piece * lanes, (piece + 1) * lanes)
        edge_ref[pl.ds(piece, edge_rows, stride=pieces)] = total[:edge_rows, across]
        node_ref[pl.ds(piece, node_rows, stride=pieces)] = total[edge_rows:, across]


def local(node_features, edge_features, open_faces, edge_weight, node_weight, cotangent):
    dims = ex, ey, nz, features = node_features.shape
    firsts, seconds = lax.axis_size("gx"), lax.axis_size("gy")
    devices = firsts * seconds
    count = ex * ey * nz

    def upward(nodes, edges, mask):
        mask = jnp.pad(mask.astype(BF16), ((0, PAD - mask.shape[0]), (0, features - mask.shape[1])))
        return jnp.concatenate([nodes.reshape(-1, features), edges.reshape(-1, features), mask], axis=0)

    above_first = passed_along(node_features[0].reshape(-1, features), "gx", -1)
    above_second = passed_along(node_features[:, 0].reshape(-1, features), "gy", -1)
    below_first = passed_along(upward(node_features[-1], edge_features[0, -1], open_faces[0, -1]), "gx", 1)
    below_second = passed_along(upward(node_features[:, -1], edge_features[1, :, -1], open_faces[1, :, -1]), "gy", 1)

    stored, other = call(
        products_kernel, [((3, count, features), F32), ((count, features), F32)], [node_features, edge_features, edge_weight]
    )
    total_rows = 4 * features
    chunk = total_rows // devices
    by_hand = (
        total_rows % devices == 0
        and chunk % 64 == 0
        and features % 128 == 0
        and firsts % 2 == 0
        and firsts & (firsts - 1) == 0
        and seconds & (seconds - 1) == 0
    )
    planes = firsts // 2
    face_first, face_second = (ey * nz, features), (ex * nz, features)
    outs = [(node_features.shape, BF16), (face_first, BF16), (face_second, BF16), (face_first, BF16), (face_second, BF16)]
    outs += [((count, features), F32)] * 2 + [(face_first, F32), (face_second, F32)] * 2
    if by_hand:
        outs += [((planes, seconds * chunk, features), BF16), ((planes, seconds * chunk, features), F32)]
        kernel = functools.partial(layer_kernel, dims)
    else:
        outs += [((total_rows, features), F32)]

        def kernel(*refs):
            layer_kernel(dims, *refs[:23], None, *refs[23:])

    low_rows = (ex + ey) * nz
    results = call(
        kernel,
        outs,
        [
            stored, other, edge_weight, node_weight, node_features, edge_features, open_faces.reshape(3 * ex * ey, nz), cotangent,
            above_first, above_second, below_first, below_second,
        ],
        scratch=[
            pltpu.VMEM((count, features), BF16),
            pltpu.VMEM((count, features), BF16),
            pltpu.VMEM((3, count, features), F32),
            pltpu.VMEM((low_rows, features), F32),
            pltpu.VMEM((3, count, features), F32),
            pltpu.VMEM((low_rows, features), F32),
            pltpu.VMEM((3 * count + low_rows, features), BF16),
            pltpu.VMEM((total_rows, features), F32),
        ],
    )
    new_nodes, low_first, low_second, top_first, top_second = results[:5]

    if by_hand:
        send, keep = results[11:]
        received = exchanged(send, "gx", 1)
    grad_above_first = passed_along(low_first, "gx", -1)
    grad_above_second = passed_along(low_second, "gy", -1)
    grad_below_first = passed_along(top_first, "gx", 1)
    grad_below_second = passed_along(top_second, "gy", 1)
    (node_grad,) = call(
        functools.partial(node_grad_kernel, dims),
        [(node_features.shape, BF16)],
        [*results[5:11], grad_above_first, grad_above_second, grad_below_first, grad_below_second, cotangent, edge_weight],
    )
    if not by_hand:
        total = results[11]
        edge_part = lax.psum_scatter(total[: 3 * features].reshape(-1), ("gx", "gy"), scatter_dimension=0, tiled=True)
        node_part = lax.psum_scatter(total[3 * features :].reshape(-1), ("gx", "gy"), scatter_dimension=0, tiled=True)
        return new_nodes, node_grad, edge_part, node_part

    block = (seconds * chunk, features)
    kept, *sends = call(pair_sum_kernel, [(block, F32)] + [(block, BF16)] * (planes - 1), [keep, received])
    arrived = [exchanged(value, "gx", 2 * (index + 1)) for index, value in enumerate(sends)]
    kept, *sends = call(
        functools.partial(plane_sum_kernel, (planes, seconds)),
        [((chunk, features), F32)] + [((chunk, features), BF16)] * (seconds - 1),
        [kept, *arrived],
    )
    arrived = [exchanged(value, "gy", index + 1) for index, value in enumerate(sends)]
    pieces = features // 128
    edge_part, node_part = call(
        last_sum_kernel, [((chunk * 3 // 4 * pieces, 128), F32), ((chunk // 4 * pieces, 128), F32)], [kept, *arrived]
    )
    return new_nodes, node_grad, edge_part.reshape(-1), node_part.reshape(-1)


def solution(mesh):
    placed = (
        P("gx", "gy", None, None),
        P(None, "gx", "gy", None, None),
        P(None, "gx", "gy", None),
        P(),
        P(),
        P("gx", "gy", None, None),
    )
    return jax.shard_map(
        local,
        mesh=mesh,
        in_specs=placed,
        out_specs=(
            P("gx", "gy", None, None),
            P("gx", "gy", None, None),
            P(("gx", "gy")),
            P(("gx", "gy")),
        ),
        check_vma=False,
    )
```

```python
import functools

import jax
import jax.numpy as jnp
from jax import lax
from jax.experimental import pallas as pl
from jax.experimental.pallas import tpu as pltpu
from jax.sharding import PartitionSpec as P

F32 = jnp.float32
BF16 = jnp.bfloat16
PAD = 16


def swapped(value, axis, first):
    count = lax.axis_size(axis)
    lower = range(first, count - 1, 2)
    return lax.ppermute(value, axis, [(at, at + 1) for at in lower] + [(at + 1, at) for at in lower])


def exchanged(value, axis, flip):
    count = lax.axis_size(axis)
    return lax.ppermute(value, axis, [(source, source ^ flip) for source in range(count)])


def dot(left, right):
    return jnp.dot(left, right, preferred_element_type=F32)


def dot_nt(left, right):
    return lax.dot_general(left, right, (((1,), (1,)), ((), ())), preferred_element_type=F32)


def dot_tn(left, right):
    return lax.dot_general(left, right, (((0,), (0,)), ((), ())), preferred_element_type=F32)


def column_of(row):
    size = row.shape[-1]
    spread = jnp.broadcast_to(row, (size, size))
    down = lax.broadcasted_iota(jnp.int32, (size, size), 0)
    across = lax.broadcasted_iota(jnp.int32, (size, size), 1)
    return jnp.sum(jnp.where(down == across, spread, 0.0), axis=1, keepdims=True)


def sigmoid(values):
    return 0.5 * jnp.tanh(0.5 * values) + 0.5


def call(kernel, outs, args, scratch=(), limit=4 << 20, cost=None):
    return pl.pallas_call(
        kernel,
        out_shape=[jax.ShapeDtypeStruct(shape, dtype) for shape, dtype in outs],
        in_specs=[pl.BlockSpec(memory_space=pltpu.VMEM)] * len(args),
        out_specs=[pl.BlockSpec(memory_space=pltpu.VMEM)] * len(outs),
        scratch_shapes=list(scratch),
        compiler_params=pltpu.CompilerParams(vmem_limit_bytes=limit),
        cost_estimate=cost,
    )(*args)


def spread_rows(rows, count):
    down = lax.broadcasted_iota(jnp.int32, (count, rows[0].shape[-1]), 0)
    tile = jnp.zeros((count, rows[0].shape[-1]), F32)
    for index, row in enumerate(rows):
        tile = jnp.where(down == index, row, tile)
    return tile


def is_even(axis):
    return lax.axis_index(axis) % 2 == 0


def pack_kernel(dims, node_ref, edge_ref, open_ref, pair_first_ref, odd_first_ref, pair_second_ref, odd_second_ref):
    ex, ey, nz, features = dims

    def fill_upward(ref, direction, cells):
        for index, (x, y) in enumerate(cells):
            ref[index * nz : (index + 1) * nz] = node_ref[x, y]
            start = (len(cells) + index) * nz
            ref[start : start + nz] = edge_ref[direction, x, y]
        mask = spread_rows([open_ref[direction, x, y : y + 1].astype(F32) for x, y in cells], PAD)
        ref[2 * len(cells) * nz :, :nz] = mask.astype(BF16)

    def fill_downward(ref, cells):
        for index, (x, y) in enumerate(cells):
            ref[index * nz : (index + 1) * nz] = node_ref[x, y]

    for direction, axis, pair_ref, odd_ref, top, low in (
        (1, "gy", pair_second_ref, odd_second_ref, [(x, ey - 1) for x in range(ex)], [(x, 0) for x in range(ex)]),
        (0, "gx", pair_first_ref, odd_first_ref, [(ex - 1, y) for y in range(ey)], [(0, y) for y in range(ey)]),
    ):
        @pl.when(is_even(axis))
        def _():
            fill_upward(pair_ref, direction, top)
            fill_downward(odd_ref, low)

        @pl.when(jnp.logical_not(is_even(axis)))
        def _():
            fill_downward(pair_ref, low)
            fill_upward(odd_ref, direction, top)


def products_kernel(node_ref, edge_ref, weight_ref, stored_ref, other_ref):
    features = node_ref.shape[-1]
    node = node_ref[...].reshape(-1, features)
    own = dot(node, weight_ref[:features])
    other_ref[...] = dot(node, weight_ref[features : 2 * features])
    for direction in range(3):
        edge = edge_ref[direction].reshape(-1, features)
        stored_ref[direction] = own + dot(edge, weight_ref[2 * features :])


def layer_kernel(
    dims,
    stored_ref, other_ref, weight_ref, node_weight_ref, node_ref, edge_ref, open_ref, cotangent_ref,
    pair_first_ref, odd_first_ref, pair_second_ref, odd_second_ref,
    new_ref, grad_odd_first_ref, grad_pair_second_ref, grad_odd_second_ref,
    own_ref, enter_ref, slope_top_first_ref, slope_top_second_ref, slope_low_first_ref, slope_low_second_ref,
    grad_pair_first_ref, send_ref, keep_ref,
    summed_ref, update_ref, slope_ref, slope_low_ref, message_ref, message_low_ref,
    grads_ref, total_ref,
):
    ex, ey, nz, features = dims
    at_first, at_second = lax.axis_index("gx"), lax.axis_index("gy")
    inside_first = (at_first < lax.axis_size("gx") - 1).astype(F32)
    inside_second = (at_second < lax.axis_size("gy") - 1).astype(F32)
    self_weight = weight_ref[:features]
    other_weight = weight_ref[features : 2 * features]
    stored_weight = weight_ref[2 * features :]

    def rows(x, y):
        return slice((x * ey + y) * nz, (x * ey + y + 1) * nz)

    def part(index):
        return slice(index * nz, (index + 1) * nz)

    def edge_terms(preact, open_column):
        gate = sigmoid(preact)
        opened = gate * open_column
        message = (preact * opened).astype(BF16).astype(F32)
        return message, opened * (1.0 + preact * (1.0 - gate))

    edge_rows_first, edge_rows_second = ey * nz, ex * nz
    even_first, even_second = is_even("gx"), is_even("gy")

    def chosen(even, pair_ref, odd_ref, start, stop):
        return jnp.where(even, odd_ref[start:stop], pair_ref[start:stop])

    node_above_first = chosen(even_first, odd_first_ref, pair_first_ref, 0, edge_rows_first)
    node_above_second = chosen(even_second, odd_second_ref, pair_second_ref, 0, edge_rows_second)
    node_below_first = chosen(even_first, pair_first_ref, odd_first_ref, 0, edge_rows_first)
    edge_below_first = chosen(even_first, pair_first_ref, odd_first_ref, edge_rows_first, 2 * edge_rows_first)
    node_below_second = chosen(even_second, pair_second_ref, odd_second_ref, 0, edge_rows_second)
    edge_below_second = chosen(even_second, pair_second_ref, odd_second_ref, edge_rows_second, 2 * edge_rows_second)
    above_first = dot(node_above_first, other_weight)
    above_second = dot(node_above_second, other_weight)
    low_first = dot(node_below_first, self_weight) + dot(edge_below_first, stored_weight)
    low_second = dot(node_below_second, self_weight) + dot(edge_below_second, stored_weight)
    mask_first = chosen(even_first, pair_first_ref, odd_first_ref, 2 * edge_rows_first, 2 * edge_rows_first + PAD).astype(F32)
    mask_second = chosen(even_second, pair_second_ref, odd_second_ref, 2 * edge_rows_second, 2 * edge_rows_second + PAD).astype(F32)
    down = lax.broadcasted_iota(jnp.int32, (nz, 1), 0)
    inside_third = jnp.where(down < nz - 1, 1.0, 0.0)

    for y in range(ey):
        message, slope = edge_terms(low_first[part(y)] + other_ref[rows(0, y)], column_of(mask_first[y : y + 1, :nz]))
        message_low_ref[part(y)] = message
        slope_low_ref[part(y)] = slope
    for x in range(ex):
        at = part(ey + x)
        message, slope = edge_terms(low_second[part(x)] + other_ref[rows(x, 0)], column_of(mask_second[x : x + 1, :nz]))
        message_low_ref[at] = message
        slope_low_ref[at] = slope
    for x in range(ex):
        for y in range(ey):
            here = rows(x, y)
            column = [
                column_of(open_ref[direction, x, y : y + 1].astype(F32)) for direction in range(3)
            ]
            if x + 1 < ex:
                beyond = other_ref[rows(x + 1, y)]
            else:
                beyond, column[0] = above_first[part(y)], column[0] * inside_first
            message_ref[0, here], slope_ref[0, here] = edge_terms(stored_ref[0, here] + beyond, column[0])
            if y + 1 < ey:
                beyond = other_ref[rows(x, y + 1)]
            else:
                beyond, column[1] = above_second[part(x)], column[1] * inside_second
            message_ref[1, here], slope_ref[1, here] = edge_terms(stored_ref[1, here] + beyond, column[1])
            beyond = pltpu.roll(other_ref[here], nz - 1, 0)
            message_ref[2, here], slope_ref[2, here] = edge_terms(stored_ref[2, here] + beyond, column[2] * inside_third)
    for x in range(ex):
        for y in range(ey):
            here = rows(x, y)
            third = message_ref[2, here]
            total = message_ref[0, here] + message_ref[1, here] + third - pltpu.roll(third, 1, 0)
            total = total - (message_ref[0, rows(x - 1, y)] if x > 0 else message_low_ref[part(y)])
            total = total - (message_ref[1, rows(x, y - 1)] if y > 0 else message_low_ref[part(ey + x)])
            summed_ref[here] = total.astype(BF16)

    node = node_ref[...].reshape(-1, features)
    update = dot(summed_ref[...], node_weight_ref[...])
    gate = sigmoid(update)
    new_ref[...] = (node.astype(F32) + update * gate).astype(BF16).reshape(new_ref.shape)
    cotangent = cotangent_ref[...].reshape(-1, features).astype(F32)
    update_ref[...] = (cotangent * (gate * (1.0 + update * (1.0 - gate)))).astype(BF16)
    grad_summed = dot_nt(update_ref[...], node_weight_ref[...]).astype(BF16)
    extra = 0 if send_ref is None else send_ref.shape[0] - edge_rows_first
    for y in range(ey):
        low, top = grad_summed[rows(0, y)], grad_summed[rows(ex - 1, y)]
        (grad_pair_first_ref if send_ref is None else send_ref)[extra + y * nz : extra + (y + 1) * nz] = jnp.where(even_first, top, low)
        grad_odd_first_ref[part(y)] = jnp.where(even_first, low, top)
    for x in range(ex):
        low, top = grad_summed[rows(x, 0)], grad_summed[rows(x, ey - 1)]
        grad_pair_second_ref[part(x)] = jnp.where(even_second, top, low)
        grad_odd_second_ref[part(x)] = jnp.where(even_second, low, top)
    wide = grad_summed.astype(F32)

    count = ex * ey * nz
    for y in range(ey):
        entering = -wide[rows(0, y)] * slope_low_ref[part(y)]
        message_low_ref[part(y)] = entering
        grads_ref[3 * count + y * nz : 3 * count + (y + 1) * nz] = entering.astype(BF16)
    for x in range(ex):
        at = part(ey + x)
        entering = -wide[rows(x, 0)] * slope_low_ref[at]
        message_low_ref[at] = entering
        start = 3 * count + (ey + x) * nz
        grads_ref[start : start + nz] = entering.astype(BF16)
    for x in range(ex):
        for y in range(ey):
            here = rows(x, y)
            mine = wide[here]
            lead = [
                mine - wide[rows(x + 1, y)] if x + 1 < ex else mine,
                mine - wide[rows(x, y + 1)] if y + 1 < ey else mine,
                mine - pltpu.roll(mine, nz - 1, 0),
            ]
            for direction in range(3):
                grad = lead[direction] * slope_ref[direction, here]
                message_ref[direction, here] = grad
                start = direction * count + (x * ey + y) * nz
                grads_ref[start : start + nz] = grad.astype(BF16)
    for x in range(ex):
        for y in range(ey):
            here = rows(x, y)
            third = message_ref[2, here]
            own_ref[here] = message_ref[0, here] + message_ref[1, here] + third
            enter = pltpu.roll(third, 1, 0)
            enter = enter + (message_ref[0, rows(x - 1, y)] if x > 0 else message_low_ref[part(y)])
            enter = enter + (message_ref[1, rows(x, y - 1)] if y > 0 else message_low_ref[part(ey + x)])
            enter_ref[here] = enter
    for y in range(ey):
        slope_top_first_ref[part(y)] = slope_ref[0, rows(ex - 1, y)]
        slope_low_first_ref[part(y)] = slope_low_ref[part(y)]
    for x in range(ex):
        slope_top_second_ref[part(x)] = slope_ref[1, rows(x, ey - 1)]
        slope_low_second_ref[part(x)] = slope_low_ref[part(ey + x)]

    grads_low = grads_ref[3 * count :]
    total_ref[:features] = dot_tn(
        jnp.concatenate([node, node_below_first, node_below_second], axis=0),
        jnp.concatenate([own_ref[...].astype(BF16), grads_low], axis=0),
    )
    tops = [grads_ref[(x * ey + y) * nz : (x * ey + y + 1) * nz] for x in [ex - 1] for y in range(ey)]
    tops += [grads_ref[count + (x * ey + y) * nz : count + (x * ey + y + 1) * nz] for x in range(ex) for y in [ey - 1]]
    total_ref[features : 2 * features] = dot_tn(
        jnp.concatenate([node, node_above_first, node_above_second], axis=0),
        jnp.concatenate([enter_ref[...].astype(BF16), *tops], axis=0),
    )
    edges = edge_ref[...].reshape(-1, features)
    total_ref[2 * features : 3 * features] = dot_tn(
        jnp.concatenate([edges, edge_below_first, edge_below_second], axis=0), grads_ref[...]
    )
    total_ref[3 * features :] = dot_tn(summed_ref[...], update_ref[...])

    if send_ref is None:
        keep_ref[...] = total_ref[...]
        return
    planes = keep_ref.shape[0]
    seconds, chunk = lax.axis_size("gy"), keep_ref.shape[1] // lax.axis_size("gy")
    edge_rows, node_rows = chunk * 3 // 4, chunk // 4
    core, plane = at_first % 2, at_first // 2
    for block in range(planes):
        for second in range(seconds):
            there = (plane ^ block) * 2
            start = second * chunk
            for flip in (core, 1 - core):
                device = (there + flip) * seconds + (at_second ^ second)
                edge = total_ref[pl.ds(pl.multiple_of(device * edge_rows, 8), edge_rows)]
                node = total_ref[pl.ds(pl.multiple_of(3 * features + device * node_rows, 8), node_rows)]
                if flip is core:
                    keep_ref[block, start : start + edge_rows] = edge
                    keep_ref[block, start + edge_rows : start + chunk] = node
                else:
                    send_at = block * seconds * chunk + start
                    send_ref[send_at : send_at + edge_rows] = edge.astype(BF16)
                    send_ref[send_at + edge_rows : send_at + chunk] = node.astype(BF16)


def node_grad_kernel(
    dims, own_ref, enter_ref, slope_top_first_ref, slope_top_second_ref, slope_low_first_ref, slope_low_second_ref,
    pair_first_ref, odd_first_ref, pair_second_ref, odd_second_ref, cotangent_ref, weight_ref, out_ref,
):
    ex, ey, nz, features = dims
    even_first, even_second = is_even("gx"), is_even("gy")
    extra = pair_first_ref.shape[0] - ey * nz

    def rows(x, y):
        return slice((x * ey + y) * nz, (x * ey + y + 1) * nz)

    def part(index):
        return slice(index * nz, (index + 1) * nz)

    own, enter = [], []
    for x in range(ex):
        for y in range(ey):
            grad = own_ref[rows(x, y)]
            pair_first = pair_first_ref[extra + y * nz : extra + (y + 1) * nz].astype(F32)
            odd_first = odd_first_ref[part(y)].astype(F32)
            pair_second, odd_second = pair_second_ref[part(x)].astype(F32), odd_second_ref[part(x)].astype(F32)
            if x == ex - 1:
                grad = grad - jnp.where(even_first, pair_first, odd_first) * slope_top_first_ref[part(y)]
            if y == ey - 1:
                grad = grad - jnp.where(even_second, pair_second, odd_second) * slope_top_second_ref[part(x)]
            own.append(grad.astype(BF16))
            grad = enter_ref[rows(x, y)]
            if x == 0:
                grad = grad + jnp.where(even_first, odd_first, pair_first) * slope_low_first_ref[part(y)]
            if y == 0:
                grad = grad + jnp.where(even_second, odd_second, pair_second) * slope_low_second_ref[part(x)]
            enter.append(grad.astype(BF16))
    result = dot_nt(jnp.concatenate(own, axis=0), weight_ref[:features])
    result = result + dot_nt(jnp.concatenate(enter, axis=0), weight_ref[features : 2 * features])
    result = result + cotangent_ref[...].reshape(-1, features).astype(F32)
    out_ref[...] = result.astype(BF16).reshape(out_ref.shape)


def pair_sum_kernel(keep_ref, received_ref, kept_ref, *send_refs):
    rows = kept_ref.shape[0]
    kept_ref[...] = keep_ref[0] + received_ref[:rows].astype(F32)
    for index, send_ref in enumerate(send_refs, 1):
        send_ref[...] = (keep_ref[index] + received_ref[index * rows : (index + 1) * rows].astype(F32)).astype(BF16)


def plane_sum_kernel(groups, keep_ref, *refs):
    received, kept_ref, send_refs = refs[: groups[0] - 1], refs[groups[0] - 1], refs[groups[0] :]
    chunk = kept_ref.shape[0]
    for index in range(groups[1]):
        here = slice(index * chunk, (index + 1) * chunk)
        total = keep_ref[here]
        for ref in received:
            total = total + ref[here].astype(F32)
        if index == 0:
            kept_ref[...] = total
        else:
            send_refs[index - 1][...] = total.astype(BF16)


def last_sum_kernel(keep_ref, *refs):
    received, edge_ref, node_ref = refs[:-2], refs[-2], refs[-1]
    total = keep_ref[...]
    for ref in received:
        total = total + ref[...].astype(F32)
    lanes = edge_ref.shape[1]
    pieces = total.shape[1] // lanes
    edge_rows, node_rows = edge_ref.shape[0] // pieces, node_ref.shape[0] // pieces
    for piece in range(pieces):
        across = slice(piece * lanes, (piece + 1) * lanes)
        edge_ref[pl.ds(piece, edge_rows, stride=pieces)] = total[:edge_rows, across]
        node_ref[pl.ds(piece, node_rows, stride=pieces)] = total[edge_rows:, across]


def local(node_features, edge_features, open_faces, edge_weight, node_weight, cotangent):
    dims = ex, ey, nz, features = node_features.shape
    firsts, seconds = lax.axis_size("gx"), lax.axis_size("gy")
    devices = firsts * seconds
    count = ex * ey * nz

    face_first, face_second = (ey * nz, features), (ex * nz, features)
    packed_first, packed_second = (2 * ey * nz + PAD, features), (2 * ex * nz + PAD, features)
    pair_first, odd_first, pair_second, odd_second = call(
        functools.partial(pack_kernel, dims),
        [(packed_first, BF16)] * 2 + [(packed_second, BF16)] * 2,
        [node_features, edge_features, open_faces],
    )
    pair_second, odd_second = swapped(pair_second, "gy", 0), swapped(odd_second, "gy", 1)
    odd_first, pair_first = swapped(odd_first, "gx", 1), swapped(pair_first, "gx", 0)

    stored, other = call(
        products_kernel, [((3, count, features), F32), ((count, features), F32)], [node_features, edge_features, edge_weight]
    )
    total_rows = 4 * features
    chunk = total_rows // devices
    by_hand = (
        total_rows % devices == 0
        and chunk % 64 == 0
        and features % 128 == 0
        and firsts % 2 == 0
        and firsts & (firsts - 1) == 0
        and seconds & (seconds - 1) == 0
    )
    planes = firsts // 2
    outs = [(node_features.shape, BF16), (face_first, BF16), (face_second, BF16), (face_second, BF16)]
    outs += [((count, features), F32)] * 2 + [(face_first, F32), (face_second, F32)] * 2
    if by_hand:
        outs += [((planes * seconds * chunk + ey * nz, features), BF16), ((planes, seconds * chunk, features), F32)]

        def kernel(*refs):
            layer_kernel(dims, *refs[:22], None, *refs[22:])

    else:
        outs += [(face_first, BF16), ((total_rows, features), F32)]

        def kernel(*refs):
            layer_kernel(dims, *refs[:23], None, *refs[23:])

    low_rows = (ex + ey) * nz
    results = call(
        kernel,
        outs,
        [
            stored, other, edge_weight, node_weight, node_features, edge_features, open_faces, cotangent,
            pair_first, odd_first, pair_second, odd_second,
        ],
        limit=16 << 20,
        scratch=[
            pltpu.VMEM((count, features), BF16),
            pltpu.VMEM((count, features), BF16),
            pltpu.VMEM((3, count, features), F32),
            pltpu.VMEM((low_rows, features), F32),
            pltpu.VMEM((3, count, features), F32),
            pltpu.VMEM((low_rows, features), F32),
            pltpu.VMEM((3 * count + low_rows, features), BF16),
            pltpu.VMEM((total_rows, features), F32),
        ],
    )
    new_nodes, odd_first, pair_second, odd_second = results[:4]
    received = swapped(results[10], "gx", 0)
    keep = results[11]
    odd_first = swapped(odd_first, "gx", 1)
    pair_second, odd_second = swapped(pair_second, "gy", 0), swapped(odd_second, "gy", 1)
    (node_grad,) = call(
        functools.partial(node_grad_kernel, dims),
        [(node_features.shape, BF16)],
        [*results[4:10], received, odd_first, pair_second, odd_second, cotangent, edge_weight],
    )
    if not by_hand:
        total = keep
        edge_part = lax.psum_scatter(total[: 3 * features].reshape(-1), ("gx", "gy"), scatter_dimension=0, tiled=True)
        node_part = lax.psum_scatter(total[3 * features :].reshape(-1), ("gx", "gy"), scatter_dimension=0, tiled=True)
        return new_nodes, node_grad, edge_part, node_part

    block = (seconds * chunk, features)
    kept, *sends = call(pair_sum_kernel, [(block, F32)] + [(block, BF16)] * (planes - 1), [keep, received])
    arrived = [exchanged(value, "gx", 2 * (index + 1)) for index, value in enumerate(sends)]
    kept, *sends = call(
        functools.partial(plane_sum_kernel, (planes, seconds)),
        [((chunk, features), F32)] + [((chunk, features), BF16)] * (seconds - 1),
        [kept, *arrived],
    )
    arrived = [exchanged(value, "gy", index + 1) for index, value in enumerate(sends)]
    pieces = features // 128
    edge_part, node_part = call(
        last_sum_kernel, [((chunk * 3 // 4 * pieces, 128), F32), ((chunk // 4 * pieces, 128), F32)], [kept, *arrived]
    )
    return new_nodes, node_grad, edge_part.reshape(-1), node_part.reshape(-1)


def solution(mesh):
    placed = (
        P("gx", "gy", None, None),
        P(None, "gx", "gy", None, None),
        P(None, "gx", "gy", None),
        P(),
        P(),
        P("gx", "gy", None, None),
    )
    return jax.shard_map(
        local,
        mesh=mesh,
        in_specs=placed,
        out_specs=(
            P("gx", "gy", None, None),
            P("gx", "gy", None, None),
            P(("gx", "gy")),
            P(("gx", "gy")),
        ),
        check_vma=False,
    )
```

```python
import functools

import jax
import jax.numpy as jnp
from jax import lax
from jax.experimental import pallas as pl
from jax.experimental.pallas import tpu as pltpu
from jax.sharding import PartitionSpec as P

F32 = jnp.float32
BF16 = jnp.bfloat16
PAD = 16


def swapped(value, axis, first):
    count = lax.axis_size(axis)
    lower = range(first, count - 1, 2)
    return lax.ppermute(value, axis, [(at, at + 1) for at in lower] + [(at + 1, at) for at in lower])


def exchanged(value, axis, flip):
    count = lax.axis_size(axis)
    return lax.ppermute(value, axis, [(source, source ^ flip) for source in range(count)])


def dot(left, right):
    return jnp.dot(left, right, preferred_element_type=F32)


def dot_nt(left, right):
    return lax.dot_general(left, right, (((1,), (1,)), ((), ())), preferred_element_type=F32)


def dot_tn(left, right):
    return lax.dot_general(left, right, (((0,), (0,)), ((), ())), preferred_element_type=F32)


def column_of(row):
    size = row.shape[-1]
    spread = jnp.broadcast_to(row, (size, size))
    down = lax.broadcasted_iota(jnp.int32, (size, size), 0)
    across = lax.broadcasted_iota(jnp.int32, (size, size), 1)
    return jnp.sum(jnp.where(down == across, spread, 0.0), axis=1, keepdims=True)


def sigmoid(values):
    return 0.5 * jnp.tanh(0.5 * values) + 0.5


def call(kernel, outs, args, scratch=(), limit=4 << 20, cost=None, far=0):
    return pl.pallas_call(
        kernel,
        out_shape=[jax.ShapeDtypeStruct(shape, dtype) for shape, dtype in outs],
        in_specs=[pl.BlockSpec(memory_space=pl.ANY)] * far + [pl.BlockSpec(memory_space=pltpu.VMEM)] * (len(args) - far),
        out_specs=[pl.BlockSpec(memory_space=pltpu.VMEM)] * len(outs),
        scratch_shapes=list(scratch),
        compiler_params=pltpu.CompilerParams(vmem_limit_bytes=limit),
        cost_estimate=cost,
    )(*args)


def spread_rows(rows, count):
    down = lax.broadcasted_iota(jnp.int32, (count, rows[0].shape[-1]), 0)
    tile = jnp.zeros((count, rows[0].shape[-1]), F32)
    for index, row in enumerate(rows):
        tile = jnp.where(down == index, row, tile)
    return tile


def is_even(axis):
    return lax.axis_index(axis) % 2 == 0


def pack_kernel(
    dims, node_ref, edge_ref, open_ref, pair_first_ref, odd_first_ref, pair_second_ref, odd_second_ref, sems
):
    ex, ey, nz, _ = dims

    def upward(ref, direction, cells):
        pairs = []
        for index, (x, y) in enumerate(cells):
            pairs.append((node_ref.at[x, y], ref.at[pl.ds(index * nz, nz)]))
            pairs.append((edge_ref.at[direction, x, y], ref.at[pl.ds((len(cells) + index) * nz, nz)]))
        return pairs

    def downward(ref, cells):
        return [(node_ref.at[x, y], ref.at[pl.ds(index * nz, nz)]) for index, (x, y) in enumerate(cells)]

    plans, used = [], 0
    for direction, axis, pair_ref, odd_ref, top, low in (
        (1, "gy", pair_second_ref, odd_second_ref, [(x, ey - 1) for x in range(ex)], [(x, 0) for x in range(ex)]),
        (0, "gx", pair_first_ref, odd_first_ref, [(ex - 1, y) for y in range(ey)], [(0, y) for y in range(ey)]),
    ):
        choices = [upward(up, direction, top) + downward(down, low) for up, down in ((pair_ref, odd_ref), (odd_ref, pair_ref))]
        copies = [
            [pltpu.make_async_copy(source, target, sems.at[used + index]) for index, (source, target) in enumerate(pairs)]
            for pairs in choices
        ]
        used += len(copies[0])
        mask = spread_rows([open_ref[direction, x, y : y + 1].astype(F32) for x, y in top], PAD).astype(BF16)
        plans.append((is_even(axis), copies, (pair_ref, odd_ref), 2 * len(top) * nz, mask))
    for even, copies, refs, start, mask in plans:
        for wanted, group in ((even, copies[0]), (jnp.logical_not(even), copies[1])):
            @pl.when(wanted)
            def _():
                for copy in group:
                    copy.start()
    for even, copies, refs, start, mask in plans:
        for ref in refs:
            ref[start:, :nz] = mask
        for wanted, group in ((even, copies[0]), (jnp.logical_not(even), copies[1])):
            @pl.when(wanted)
            def _():
                for copy in group:
                    copy.wait()


def edge_terms(preact, open_column):
    gate = sigmoid(preact)
    opened = gate * open_column
    message = (preact * opened).astype(BF16).astype(F32)
    return message, opened * (1.0 + preact * (1.0 - gate))


def halves(even, pair_ref, odd_ref, rows):
    def pick(first, second, start, stop):
        return jnp.where(even, first[start:stop], second[start:stop])

    return (
        pick(pair_ref, odd_ref, 0, rows),
        pick(odd_ref, pair_ref, 0, rows),
        pick(odd_ref, pair_ref, rows, 2 * rows),
        pick(odd_ref, pair_ref, 2 * rows, 2 * rows + PAD).astype(F32),
    )


def before_kernel(
    dims, node_ref, edge_ref, open_ref, weight_ref,
    sum_ref, slope_ref, stored_top_first_ref, other_low_first_ref, stored_top_second_ref, other_low_second_ref,
    other_ref, stored_ref, message_ref,
):
    ex, ey, nz, features = dims

    def rows(x, y):
        return slice((x * ey + y) * nz, (x * ey + y + 1) * nz)

    def part(index):
        return slice(index * nz, (index + 1) * nz)

    node = node_ref[...].reshape(-1, features)
    own = dot(node, weight_ref[:features])
    other_ref[...] = dot(node, weight_ref[features : 2 * features])
    for direction in range(3):
        stored_ref[direction] = own + dot(edge_ref[direction].reshape(-1, features), weight_ref[2 * features :])
    inside_third = jnp.where(lax.broadcasted_iota(jnp.int32, (nz, 1), 0) < nz - 1, 1.0, 0.0)
    for y in range(ey):
        stored_top_first_ref[part(y)] = stored_ref[0, rows(ex - 1, y)]
        other_low_first_ref[part(y)] = other_ref[rows(0, y)]
    for x in range(ex):
        stored_top_second_ref[part(x)] = stored_ref[1, rows(x, ey - 1)]
        other_low_second_ref[part(x)] = other_ref[rows(x, 0)]
        for y in range(ey):
            here = rows(x, y)
            column = [column_of(open_ref[direction, x, y : y + 1].astype(F32)) for direction in range(3)]
            if x + 1 < ex:
                beyond = other_ref[rows(x + 1, y)]
                message_ref[0, here], slope_ref[0, here] = edge_terms(stored_ref[0, here] + beyond, column[0])
            if y + 1 < ey:
                beyond = other_ref[rows(x, y + 1)]
                message_ref[1, here], slope_ref[1, here] = edge_terms(stored_ref[1, here] + beyond, column[1])
            beyond = pltpu.roll(other_ref[here], nz - 1, 0)
            message_ref[2, here], slope_ref[2, here] = edge_terms(stored_ref[2, here] + beyond, column[2] * inside_third)
    for x in range(ex):
        for y in range(ey):
            here = rows(x, y)
            third = message_ref[2, here]
            total = third - pltpu.roll(third, 1, 0)
            if x + 1 < ex:
                total = total + message_ref[0, here]
            if x > 0:
                total = total - message_ref[0, rows(x - 1, y)]
            if y + 1 < ey:
                total = total + message_ref[1, here]
            if y > 0:
                total = total - message_ref[1, rows(x, y - 1)]
            sum_ref[here] = total


def layer_kernel(
    dims,
    sum_ref, slope_ref, stored_top_first_ref, other_low_first_ref, stored_top_second_ref, other_low_second_ref,
    weight_ref, node_weight_ref, node_ref, edge_ref, open_ref, cotangent_ref,
    pair_first_ref, odd_first_ref, pair_second_ref, odd_second_ref,
    new_ref, grad_odd_first_ref, grad_pair_second_ref, grad_odd_second_ref,
    own_ref, enter_ref, slope_top_first_ref, slope_low_first_ref, slope_top_second_ref, slope_low_second_ref,
    grad_pair_first_ref, send_ref, keep_ref,
    summed_ref, update_ref, grad_ref, grad_low_ref, grads_ref, total_ref,
):
    ex, ey, nz, features = dims
    at_first, at_second = lax.axis_index("gx"), lax.axis_index("gy")
    inside_first = (at_first < lax.axis_size("gx") - 1).astype(F32)
    inside_second = (at_second < lax.axis_size("gy") - 1).astype(F32)
    even_first, even_second = is_even("gx"), is_even("gy")

    def rows(x, y):
        return slice((x * ey + y) * nz, (x * ey + y + 1) * nz)

    def part(index):
        return slice(index * nz, (index + 1) * nz)

    rows_first, rows_second = ey * nz, ex * nz
    node_above_first, node_below_first, edge_below_first, mask_first = halves(
        even_first, pair_first_ref, odd_first_ref, rows_first
    )
    node_above_second, node_below_second, edge_below_second, mask_second = halves(
        even_second, pair_second_ref, odd_second_ref, rows_second
    )
    other_weight = weight_ref[features : 2 * features]
    above_first, above_second = dot(node_above_first, other_weight), dot(node_above_second, other_weight)
    entering_first = dot(node_below_first, weight_ref[:features]) + dot(edge_below_first, weight_ref[2 * features :])
    entering_second = dot(node_below_second, weight_ref[:features]) + dot(edge_below_second, weight_ref[2 * features :])
    totals = [[sum_ref[rows(x, y)] for y in range(ey)] for x in range(ex)]
    for y in range(ey):
        here = part(y)
        column = column_of(open_ref[0, ex - 1, y : y + 1].astype(F32)) * inside_first
        message, slope_top_first_ref[here] = edge_terms(stored_top_first_ref[here] + above_first[here], column)
        totals[ex - 1][y] = totals[ex - 1][y] + message
        column = column_of(mask_first[y : y + 1, :nz])
        message, slope_low_first_ref[here] = edge_terms(entering_first[here] + other_low_first_ref[here], column)
        totals[0][y] = totals[0][y] - message
    for x in range(ex):
        here = part(x)
        column = column_of(open_ref[1, x, ey - 1 : ey].astype(F32)) * inside_second
        message, slope_top_second_ref[here] = edge_terms(stored_top_second_ref[here] + above_second[here], column)
        totals[x][ey - 1] = totals[x][ey - 1] + message
        column = column_of(mask_second[x : x + 1, :nz])
        message, slope_low_second_ref[here] = edge_terms(entering_second[here] + other_low_second_ref[here], column)
        totals[x][0] = totals[x][0] - message
    for x in range(ex):
        for y in range(ey):
            summed_ref[rows(x, y)] = totals[x][y].astype(BF16)

    node = node_ref[...].reshape(-1, features)
    update = dot(summed_ref[...], node_weight_ref[...])
    gate = sigmoid(update)
    new_ref[...] = (node.astype(F32) + update * gate).astype(BF16).reshape(new_ref.shape)
    cotangent = cotangent_ref[...].reshape(-1, features).astype(F32)
    update_ref[...] = (cotangent * (gate * (1.0 + update * (1.0 - gate)))).astype(BF16)
    grad_summed = dot_nt(update_ref[...], node_weight_ref[...]).astype(BF16)
    pair_target, extra = (grad_pair_first_ref, 0) if send_ref is None else (send_ref, send_ref.shape[0] - rows_first)
    for y in range(ey):
        low, top = grad_summed[rows(0, y)], grad_summed[rows(ex - 1, y)]
        pair_target[extra + y * nz : extra + (y + 1) * nz] = jnp.where(even_first, top, low)
        grad_odd_first_ref[part(y)] = jnp.where(even_first, low, top)
    for x in range(ex):
        low, top = grad_summed[rows(x, 0)], grad_summed[rows(x, ey - 1)]
        grad_pair_second_ref[part(x)] = jnp.where(even_second, top, low)
        grad_odd_second_ref[part(x)] = jnp.where(even_second, low, top)
    wide = grad_summed.astype(F32)

    count = ex * ey * nz
    for index in range(ey + ex):
        cell = rows(0, index) if index < ey else rows(index - ey, 0)
        slope = slope_low_first_ref[part(index)] if index < ey else slope_low_second_ref[part(index - ey)]
        grad = -wide[cell] * slope
        grad_low_ref[part(index)] = grad
        grads_ref[3 * count + index * nz : 3 * count + (index + 1) * nz] = grad.astype(BF16)
    for x in range(ex):
        for y in range(ey):
            here = rows(x, y)
            mine = wide[here]
            lead = [
                mine - wide[rows(x + 1, y)] if x + 1 < ex else mine,
                mine - wide[rows(x, y + 1)] if y + 1 < ey else mine,
                mine - pltpu.roll(mine, nz - 1, 0),
            ]
            for direction in range(3):
                if direction == 0 and x == ex - 1:
                    slope = slope_top_first_ref[part(y)]
                elif direction == 1 and y == ey - 1:
                    slope = slope_top_second_ref[part(x)]
                else:
                    slope = slope_ref[direction, here]
                grad = lead[direction] * slope
                grad_ref[direction, here] = grad
                start = direction * count + (x * ey + y) * nz
                grads_ref[start : start + nz] = grad.astype(BF16)
    for x in range(ex):
        for y in range(ey):
            here = rows(x, y)
            third = grad_ref[2, here]
            own_ref[here] = grad_ref[0, here] + grad_ref[1, here] + third
            enter = pltpu.roll(third, 1, 0)
            enter = enter + (grad_ref[0, rows(x - 1, y)] if x > 0 else grad_low_ref[part(y)])
            enter = enter + (grad_ref[1, rows(x, y - 1)] if y > 0 else grad_low_ref[part(ey + x)])
            enter_ref[here] = enter

    grads_low = grads_ref[3 * count :]
    total_ref[:features] = dot_tn(
        jnp.concatenate([node, node_below_first, node_below_second], axis=0),
        jnp.concatenate([own_ref[...].astype(BF16), grads_low], axis=0),
    )
    tops = [grads_ref[((ex - 1) * ey + y) * nz : ((ex - 1) * ey + y + 1) * nz] for y in range(ey)]
    tops += [grads_ref[count + (x * ey + ey - 1) * nz : count + (x * ey + ey) * nz] for x in range(ex)]
    total_ref[features : 2 * features] = dot_tn(
        jnp.concatenate([node, node_above_first, node_above_second], axis=0),
        jnp.concatenate([enter_ref[...].astype(BF16), *tops], axis=0),
    )
    edges = edge_ref[...].reshape(-1, features)
    total_ref[2 * features : 3 * features] = dot_tn(
        jnp.concatenate([edges, edge_below_first, edge_below_second], axis=0), grads_ref[...]
    )
    total_ref[3 * features :] = dot_tn(summed_ref[...], update_ref[...])

    if send_ref is None:
        keep_ref[...] = total_ref[...]
        return
    planes = keep_ref.shape[0]
    seconds, chunk = lax.axis_size("gy"), keep_ref.shape[1] // lax.axis_size("gy")
    edge_rows, node_rows = chunk * 3 // 4, chunk // 4
    core, plane = at_first % 2, at_first // 2
    for block in range(planes):
        for second in range(seconds):
            there = (plane ^ block) * 2
            start = second * chunk
            for flip in (core, 1 - core):
                device = (there + flip) * seconds + (at_second ^ second)
                edge = total_ref[pl.ds(pl.multiple_of(device * edge_rows, 8), edge_rows)]
                node = total_ref[pl.ds(pl.multiple_of(3 * features + device * node_rows, 8), node_rows)]
                if flip is core:
                    keep_ref[block, start : start + edge_rows] = edge
                    keep_ref[block, start + edge_rows : start + chunk] = node
                else:
                    send_at = block * seconds * chunk + start
                    send_ref[send_at : send_at + edge_rows] = edge.astype(BF16)
                    send_ref[send_at + edge_rows : send_at + chunk] = node.astype(BF16)


def node_grad_kernel(
    dims, own_ref, enter_ref, slope_top_first_ref, slope_low_first_ref, slope_top_second_ref, slope_low_second_ref,
    pair_first_ref, odd_first_ref, pair_second_ref, odd_second_ref, cotangent_ref, weight_ref, out_ref,
):
    ex, ey, nz, features = dims
    even_first, even_second = is_even("gx"), is_even("gy")
    extra = pair_first_ref.shape[0] - ey * nz

    def rows(x, y):
        return slice((x * ey + y) * nz, (x * ey + y + 1) * nz)

    def part(index):
        return slice(index * nz, (index + 1) * nz)

    own, enter = [], []
    for x in range(ex):
        for y in range(ey):
            grad = own_ref[rows(x, y)]
            pair_first = pair_first_ref[extra + y * nz : extra + (y + 1) * nz].astype(F32)
            odd_first = odd_first_ref[part(y)].astype(F32)
            pair_second, odd_second = pair_second_ref[part(x)].astype(F32), odd_second_ref[part(x)].astype(F32)
            if x == ex - 1:
                grad = grad - jnp.where(even_first, pair_first, odd_first) * slope_top_first_ref[part(y)]
            if y == ey - 1:
                grad = grad - jnp.where(even_second, pair_second, odd_second) * slope_top_second_ref[part(x)]
            own.append(grad.astype(BF16))
            grad = enter_ref[rows(x, y)]
            if x == 0:
                grad = grad + jnp.where(even_first, odd_first, pair_first) * slope_low_first_ref[part(y)]
            if y == 0:
                grad = grad + jnp.where(even_second, odd_second, pair_second) * slope_low_second_ref[part(x)]
            enter.append(grad.astype(BF16))
    result = dot_nt(jnp.concatenate(own, axis=0), weight_ref[:features])
    result = result + dot_nt(jnp.concatenate(enter, axis=0), weight_ref[features : 2 * features])
    result = result + cotangent_ref[...].reshape(-1, features).astype(F32)
    out_ref[...] = result.astype(BF16).reshape(out_ref.shape)


def pair_sum_kernel(keep_ref, received_ref, kept_ref, *send_refs):
    rows = kept_ref.shape[0]
    kept_ref[...] = keep_ref[0] + received_ref[:rows].astype(F32)
    for index, send_ref in enumerate(send_refs, 1):
        send_ref[...] = (keep_ref[index] + received_ref[index * rows : (index + 1) * rows].astype(F32)).astype(BF16)


def plane_sum_kernel(groups, keep_ref, *refs):
    received, kept_ref, send_refs = refs[: groups[0] - 1], refs[groups[0] - 1], refs[groups[0] :]
    chunk = kept_ref.shape[0]
    for index in range(groups[1]):
        here = slice(index * chunk, (index + 1) * chunk)
        total = keep_ref[here]
        for ref in received:
            total = total + ref[here].astype(F32)
        if index == 0:
            kept_ref[...] = total
        else:
            send_refs[index - 1][...] = total.astype(BF16)


def last_sum_kernel(keep_ref, *refs):
    received, edge_ref, node_ref = refs[:-2], refs[-2], refs[-1]
    total = keep_ref[...]
    for ref in received:
        total = total + ref[...].astype(F32)
    lanes = edge_ref.shape[1]
    pieces = total.shape[1] // lanes
    edge_rows, node_rows = edge_ref.shape[0] // pieces, node_ref.shape[0] // pieces
    for piece in range(pieces):
        across = slice(piece * lanes, (piece + 1) * lanes)
        edge_ref[pl.ds(piece, edge_rows, stride=pieces)] = total[:edge_rows, across]
        node_ref[pl.ds(piece, node_rows, stride=pieces)] = total[edge_rows:, across]


def local(node_features, edge_features, open_faces, edge_weight, node_weight, cotangent):
    dims = ex, ey, nz, features = node_features.shape
    firsts, seconds = lax.axis_size("gx"), lax.axis_size("gy")
    devices = firsts * seconds
    count = ex * ey * nz

    face_first, face_second = (ey * nz, features), (ex * nz, features)
    packed_first, packed_second = (2 * ey * nz + PAD, features), (2 * ex * nz + PAD, features)
    copies = 3 * (ex + ey)
    pair_first, odd_first, pair_second, odd_second = call(
        functools.partial(pack_kernel, dims),
        [(packed_first, BF16)] * 2 + [(packed_second, BF16)] * 2,
        [node_features, edge_features, open_faces],
        scratch=[pltpu.SemaphoreType.DMA((copies,))],
        far=2,
    )
    pair_second = swapped(pair_second, "gy", 0)
    odd_second = swapped(odd_second, "gy", 1)
    odd_first = swapped(odd_first, "gx", 1)
    pair_first = swapped(pair_first, "gx", 0)
    before = [((count, features), F32), ((3, count, features), F32)] + [(face_first, F32)] * 2 + [(face_second, F32)] * 2
    before = call(
        functools.partial(before_kernel, dims),
        before,
        [node_features, edge_features, open_faces, edge_weight],
        scratch=[
            pltpu.VMEM((count, features), F32),
            pltpu.VMEM((3, count, features), F32),
            pltpu.VMEM((3, count, features), F32),
        ],
        limit=12 << 20,
    )
    total_rows = 4 * features
    chunk = total_rows // devices
    by_hand = (
        total_rows % devices == 0
        and chunk % 64 == 0
        and features % 128 == 0
        and firsts % 2 == 0
        and firsts & (firsts - 1) == 0
        and seconds & (seconds - 1) == 0
    )
    planes = firsts // 2
    outs = [(node_features.shape, BF16), (face_first, BF16), (face_second, BF16), (face_second, BF16)]
    outs += [((count, features), F32)] * 2 + [(face_first, F32)] * 2 + [(face_second, F32)] * 2
    if by_hand:
        outs += [((planes * seconds * chunk + ey * nz, features), BF16), ((planes, seconds * chunk, features), F32)]

        def kernel(*refs):
            layer_kernel(dims, *refs[:26], None, *refs[26:])

    else:
        outs += [(face_first, BF16), ((total_rows, features), F32)]

        def kernel(*refs):
            layer_kernel(dims, *refs[:27], None, *refs[27:])

    low_rows = (ex + ey) * nz
    results = call(
        kernel,
        outs,
        [
            *before, edge_weight, node_weight, node_features, edge_features, open_faces, cotangent,
            pair_first, odd_first, pair_second, odd_second,
        ],
        scratch=[
            pltpu.VMEM((count, features), BF16),
            pltpu.VMEM((count, features), BF16),
            pltpu.VMEM((3, count, features), F32),
            pltpu.VMEM((low_rows, features), F32),
            pltpu.VMEM((3 * count + low_rows, features), BF16),
            pltpu.VMEM((total_rows, features), F32),
        ],
        limit=14 << 20,
    )
    new_nodes, odd_first, pair_second, odd_second = results[:4]
    received, keep = results[10:]
    received = swapped(received, "gx", 0)
    pair_second = swapped(pair_second, "gy", 0)
    odd_second = swapped(odd_second, "gy", 1)
    odd_first = swapped(odd_first, "gx", 1)
    (node_grad,) = call(
        functools.partial(node_grad_kernel, dims),
        [(node_features.shape, BF16)],
        [
            *results[4:10], received, odd_first, pair_second, odd_second, cotangent, edge_weight,
        ],
    )
    if not by_hand:
        total = keep
        edge_part = lax.psum_scatter(total[: 3 * features].reshape(-1), ("gx", "gy"), scatter_dimension=0, tiled=True)
        node_part = lax.psum_scatter(total[3 * features :].reshape(-1), ("gx", "gy"), scatter_dimension=0, tiled=True)
        return new_nodes, node_grad, edge_part, node_part

    block = (seconds * chunk, features)
    kept, *sends = call(pair_sum_kernel, [(block, F32)] + [(block, BF16)] * (planes - 1), [keep, received])
    arrived = []
    for index, value in enumerate(sends):
        arrived.append(exchanged(value, "gx", 2 * (index + 1)))
    kept, *sends = call(
        functools.partial(plane_sum_kernel, (planes, seconds)),
        [((chunk, features), F32)] + [((chunk, features), BF16)] * (seconds - 1),
        [kept, *arrived],
    )
    arrived = []
    for index, value in enumerate(sends):
        arrived.append(exchanged(value, "gy", index + 1))
    pieces = features // 128
    edge_part, node_part = call(
        last_sum_kernel, [((chunk * 3 // 4 * pieces, 128), F32), ((chunk // 4 * pieces, 128), F32)], [kept, *arrived]
    )
    return new_nodes, node_grad, edge_part.reshape(-1), node_part.reshape(-1)


def solution(mesh):
    placed = (
        P("gx", "gy", None, None),
        P(None, "gx", "gy", None, None),
        P(None, "gx", "gy", None),
        P(),
        P(),
        P("gx", "gy", None, None),
    )
    return jax.shard_map(
        local,
        mesh=mesh,
        in_specs=placed,
        out_specs=(
            P("gx", "gy", None, None),
            P("gx", "gy", None, None),
            P(("gx", "gy")),
            P(("gx", "gy")),
        ),
        check_vma=False,
    )
```

```python
import functools

import jax
import jax.numpy as jnp
from jax import lax
from jax.experimental import pallas as pl
from jax.experimental.pallas import tpu as pltpu
from jax.sharding import PartitionSpec as P

F32 = jnp.float32
BF16 = jnp.bfloat16
PAD = 16


def swapped(value, axis, first):
    count = lax.axis_size(axis)
    lower = range(first, count - 1, 2)
    return lax.ppermute(value, axis, [(at, at + 1) for at in lower] + [(at + 1, at) for at in lower])


def exchanged(value, axis, flip):
    count = lax.axis_size(axis)
    return lax.ppermute(value, axis, [(source, source ^ flip) for source in range(count)])


def dot(left, right):
    return jnp.dot(left, right, preferred_element_type=F32)


def dot_nt(left, right):
    return lax.dot_general(left, right, (((1,), (1,)), ((), ())), preferred_element_type=F32)


def dot_tn(left, right):
    return lax.dot_general(left, right, (((0,), (0,)), ((), ())), preferred_element_type=F32)


def column_of(row):
    size = row.shape[-1]
    spread = jnp.broadcast_to(row, (size, size))
    down = lax.broadcasted_iota(jnp.int32, (size, size), 0)
    across = lax.broadcasted_iota(jnp.int32, (size, size), 1)
    return jnp.sum(jnp.where(down == across, spread, 0.0), axis=1, keepdims=True)


def sigmoid(values):
    return 0.5 * jnp.tanh(0.5 * values) + 0.5


def call(kernel, outs, args, scratch=(), limit=4 << 20, cost=None, far=0):
    args = [pltpu.with_memory_space_constraint(arg, pltpu.HBM) for arg in args[:far]] + list(args[far:])
    return pl.pallas_call(
        kernel,
        out_shape=[jax.ShapeDtypeStruct(shape, dtype) for shape, dtype in outs],
        in_specs=[pl.BlockSpec(memory_space=pltpu.HBM)] * far + [pl.BlockSpec(memory_space=pltpu.VMEM)] * (len(args) - far),
        out_specs=[pl.BlockSpec(memory_space=pltpu.VMEM)] * len(outs),
        scratch_shapes=list(scratch),
        compiler_params=pltpu.CompilerParams(vmem_limit_bytes=limit),
        cost_estimate=cost,
    )(*args)


def spread_rows(rows, count):
    down = lax.broadcasted_iota(jnp.int32, (count, rows[0].shape[-1]), 0)
    tile = jnp.zeros((count, rows[0].shape[-1]), F32)
    for index, row in enumerate(rows):
        tile = jnp.where(down == index, row, tile)
    return tile


def is_even(axis):
    return lax.axis_index(axis) % 2 == 0


def pack_kernel(
    dims, node_ref, edge_ref, faces_ref, pair_first_ref, odd_first_ref, pair_second_ref, odd_second_ref, open_ref, sems
):
    ex, ey, nz, _ = dims
    faces_copy = pltpu.make_async_copy(faces_ref, open_ref, sems.at[0])
    faces_copy.start()

    def upward(ref, direction, cells):
        pairs = []
        for index, (x, y) in enumerate(cells):
            pairs.append((node_ref.at[x, y], ref.at[pl.ds(index * nz, nz)]))
            pairs.append((edge_ref.at[direction, x, y], ref.at[pl.ds((len(cells) + index) * nz, nz)]))
        return pairs

    def downward(ref, cells):
        return [(node_ref.at[x, y], ref.at[pl.ds(index * nz, nz)]) for index, (x, y) in enumerate(cells)]

    plans, used = [], 1
    for direction, axis, pair_ref, odd_ref, top, low in (
        (1, "gy", pair_second_ref, odd_second_ref, [(x, ey - 1) for x in range(ex)], [(x, 0) for x in range(ex)]),
        (0, "gx", pair_first_ref, odd_first_ref, [(ex - 1, y) for y in range(ey)], [(0, y) for y in range(ey)]),
    ):
        choices = [upward(up, direction, top) + downward(down, low) for up, down in ((pair_ref, odd_ref), (odd_ref, pair_ref))]
        copies = [
            [pltpu.make_async_copy(source, target, sems.at[used + index]) for index, (source, target) in enumerate(pairs)]
            for pairs in choices
        ]
        used += len(copies[0])
        plans.append((is_even(axis), copies, (pair_ref, odd_ref), 2 * len(top) * nz, (direction, top)))
    for even, copies, _, _, _ in plans:
        for wanted, group in ((even, copies[0]), (jnp.logical_not(even), copies[1])):
            @pl.when(wanted)
            def _():
                for copy in group:
                    copy.start()
    faces_copy.wait()
    for even, copies, refs, start, (direction, top) in plans:
        mask = spread_rows([open_ref[direction, x, y : y + 1].astype(F32) for x, y in top], PAD).astype(BF16)
        for ref in refs:
            ref[start:, :nz] = mask
        for wanted, group in ((even, copies[0]), (jnp.logical_not(even), copies[1])):
            @pl.when(wanted)
            def _():
                for copy in group:
                    copy.wait()


def edge_terms(preact, open_column):
    gate = sigmoid(preact)
    opened = gate * open_column
    message = (preact * opened).astype(BF16).astype(F32)
    return message, opened * (1.0 + preact * (1.0 - gate))


def halves(even, pair_ref, odd_ref, rows):
    def pick(first, second, start, stop):
        return jnp.where(even, first[start:stop], second[start:stop])

    return (
        pick(pair_ref, odd_ref, 0, rows),
        pick(odd_ref, pair_ref, 0, rows),
        pick(odd_ref, pair_ref, rows, 2 * rows),
        pick(odd_ref, pair_ref, 2 * rows, 2 * rows + PAD).astype(F32),
    )


def before_kernel(
    dims, node_ref, edge_ref, weight_ref, faces_ref,
    sum_ref, slope_ref, stored_top_first_ref, other_low_first_ref, stored_top_second_ref, other_low_second_ref,
    other_ref, stored_ref, message_ref, node_here, edge_here, weight_here, open_ref, sems,
):
    ex, ey, nz, features = dims
    copies = [
        pltpu.make_async_copy(node_ref, node_here, sems.at[0]),
        pltpu.make_async_copy(weight_ref, weight_here, sems.at[1]),
        pltpu.make_async_copy(edge_ref, edge_here, sems.at[2]),
        pltpu.make_async_copy(faces_ref, open_ref, sems.at[3]),
    ]
    for copy in copies:
        copy.start()

    def rows(x, y):
        return slice((x * ey + y) * nz, (x * ey + y + 1) * nz)

    def part(index):
        return slice(index * nz, (index + 1) * nz)

    copies[0].wait()
    copies[1].wait()
    node = node_here[...].reshape(-1, features)
    own = dot(node, weight_here[:features])
    other_ref[...] = dot(node, weight_here[features : 2 * features])
    copies[2].wait()
    copies[3].wait()
    for direction in range(3):
        stored_ref[direction] = own + dot(edge_here[direction].reshape(-1, features), weight_here[2 * features :])
    inside_third = jnp.where(lax.broadcasted_iota(jnp.int32, (nz, 1), 0) < nz - 1, 1.0, 0.0)
    for y in range(ey):
        stored_top_first_ref[part(y)] = stored_ref[0, rows(ex - 1, y)]
        other_low_first_ref[part(y)] = other_ref[rows(0, y)]
    for x in range(ex):
        stored_top_second_ref[part(x)] = stored_ref[1, rows(x, ey - 1)]
        other_low_second_ref[part(x)] = other_ref[rows(x, 0)]
        for y in range(ey):
            here = rows(x, y)
            column = [column_of(open_ref[direction, x, y : y + 1].astype(F32)) for direction in range(3)]
            if x + 1 < ex:
                beyond = other_ref[rows(x + 1, y)]
                message_ref[0, here], slope_ref[0, here] = edge_terms(stored_ref[0, here] + beyond, column[0])
            if y + 1 < ey:
                beyond = other_ref[rows(x, y + 1)]
                message_ref[1, here], slope_ref[1, here] = edge_terms(stored_ref[1, here] + beyond, column[1])
            beyond = pltpu.roll(other_ref[here], nz - 1, 0)
            message_ref[2, here], slope_ref[2, here] = edge_terms(stored_ref[2, here] + beyond, column[2] * inside_third)
    for x in range(ex):
        for y in range(ey):
            here = rows(x, y)
            third = message_ref[2, here]
            total = third - pltpu.roll(third, 1, 0)
            if x + 1 < ex:
                total = total + message_ref[0, here]
            if x > 0:
                total = total - message_ref[0, rows(x - 1, y)]
            if y + 1 < ey:
                total = total + message_ref[1, here]
            if y > 0:
                total = total - message_ref[1, rows(x, y - 1)]
            sum_ref[here] = total


def layer_kernel(
    dims,
    sum_ref, slope_ref, stored_top_first_ref, other_low_first_ref, stored_top_second_ref, other_low_second_ref,
    weight_ref, node_weight_ref, node_ref, edge_ref, open_ref, cotangent_ref,
    pair_first_ref, odd_first_ref, pair_second_ref, odd_second_ref,
    new_ref, grad_odd_first_ref, grad_pair_second_ref, grad_odd_second_ref,
    own_ref, enter_ref, slope_top_first_ref, slope_low_first_ref, slope_top_second_ref, slope_low_second_ref,
    grad_pair_first_ref, send_ref, keep_ref,
    summed_ref, update_ref, grad_ref, grad_low_ref, grads_ref, total_ref,
):
    ex, ey, nz, features = dims
    at_first, at_second = lax.axis_index("gx"), lax.axis_index("gy")
    inside_first = (at_first < lax.axis_size("gx") - 1).astype(F32)
    inside_second = (at_second < lax.axis_size("gy") - 1).astype(F32)
    even_first, even_second = is_even("gx"), is_even("gy")

    def rows(x, y):
        return slice((x * ey + y) * nz, (x * ey + y + 1) * nz)

    def part(index):
        return slice(index * nz, (index + 1) * nz)

    rows_first, rows_second = ey * nz, ex * nz
    node_above_first, node_below_first, edge_below_first, mask_first = halves(
        even_first, pair_first_ref, odd_first_ref, rows_first
    )
    node_above_second, node_below_second, edge_below_second, mask_second = halves(
        even_second, pair_second_ref, odd_second_ref, rows_second
    )
    other_weight = weight_ref[features : 2 * features]
    above_first, above_second = dot(node_above_first, other_weight), dot(node_above_second, other_weight)
    entering_first = dot(node_below_first, weight_ref[:features]) + dot(edge_below_first, weight_ref[2 * features :])
    entering_second = dot(node_below_second, weight_ref[:features]) + dot(edge_below_second, weight_ref[2 * features :])
    totals = [[sum_ref[rows(x, y)] for y in range(ey)] for x in range(ex)]
    for y in range(ey):
        here = part(y)
        column = column_of(open_ref[0, ex - 1, y : y + 1].astype(F32)) * inside_first
        message, slope_top_first_ref[here] = edge_terms(stored_top_first_ref[here] + above_first[here], column)
        totals[ex - 1][y] = totals[ex - 1][y] + message
        column = column_of(mask_first[y : y + 1, :nz])
        message, slope_low_first_ref[here] = edge_terms(entering_first[here] + other_low_first_ref[here], column)
        totals[0][y] = totals[0][y] - message
    for x in range(ex):
        here = part(x)
        column = column_of(open_ref[1, x, ey - 1 : ey].astype(F32)) * inside_second
        message, slope_top_second_ref[here] = edge_terms(stored_top_second_ref[here] + above_second[here], column)
        totals[x][ey - 1] = totals[x][ey - 1] + message
        column = column_of(mask_second[x : x + 1, :nz])
        message, slope_low_second_ref[here] = edge_terms(entering_second[here] + other_low_second_ref[here], column)
        totals[x][0] = totals[x][0] - message
    for x in range(ex):
        for y in range(ey):
            summed_ref[rows(x, y)] = totals[x][y].astype(BF16)

    node = node_ref[...].reshape(-1, features)
    update = dot(summed_ref[...], node_weight_ref[...])
    gate = sigmoid(update)
    new_ref[...] = (node.astype(F32) + update * gate).astype(BF16).reshape(new_ref.shape)
    cotangent = cotangent_ref[...].reshape(-1, features).astype(F32)
    update_ref[...] = (cotangent * (gate * (1.0 + update * (1.0 - gate)))).astype(BF16)
    grad_summed = dot_nt(update_ref[...], node_weight_ref[...]).astype(BF16)
    pair_target, extra = (grad_pair_first_ref, 0) if send_ref is None else (send_ref, send_ref.shape[0] - rows_first)
    for y in range(ey):
        low, top = grad_summed[rows(0, y)], grad_summed[rows(ex - 1, y)]
        pair_target[extra + y * nz : extra + (y + 1) * nz] = jnp.where(even_first, top, low)
        grad_odd_first_ref[part(y)] = jnp.where(even_first, low, top)
    for x in range(ex):
        low, top = grad_summed[rows(x, 0)], grad_summed[rows(x, ey - 1)]
        grad_pair_second_ref[part(x)] = jnp.where(even_second, top, low)
        grad_odd_second_ref[part(x)] = jnp.where(even_second, low, top)
    wide = grad_summed.astype(F32)

    count = ex * ey * nz
    for index in range(ey + ex):
        cell = rows(0, index) if index < ey else rows(index - ey, 0)
        slope = slope_low_first_ref[part(index)] if index < ey else slope_low_second_ref[part(index - ey)]
        grad = -wide[cell] * slope
        grad_low_ref[part(index)] = grad
        grads_ref[3 * count + index * nz : 3 * count + (index + 1) * nz] = grad.astype(BF16)
    for x in range(ex):
        for y in range(ey):
            here = rows(x, y)
            mine = wide[here]
            lead = [
                mine - wide[rows(x + 1, y)] if x + 1 < ex else mine,
                mine - wide[rows(x, y + 1)] if y + 1 < ey else mine,
                mine - pltpu.roll(mine, nz - 1, 0),
            ]
            for direction in range(3):
                if direction == 0 and x == ex - 1:
                    slope = slope_top_first_ref[part(y)]
                elif direction == 1 and y == ey - 1:
                    slope = slope_top_second_ref[part(x)]
                else:
                    slope = slope_ref[direction, here]
                grad = lead[direction] * slope
                grad_ref[direction, here] = grad
                start = direction * count + (x * ey + y) * nz
                grads_ref[start : start + nz] = grad.astype(BF16)
    for x in range(ex):
        for y in range(ey):
            here = rows(x, y)
            third = grad_ref[2, here]
            own_ref[here] = grad_ref[0, here] + grad_ref[1, here] + third
            enter = pltpu.roll(third, 1, 0)
            enter = enter + (grad_ref[0, rows(x - 1, y)] if x > 0 else grad_low_ref[part(y)])
            enter = enter + (grad_ref[1, rows(x, y - 1)] if y > 0 else grad_low_ref[part(ey + x)])
            enter_ref[here] = enter

    grads_low = grads_ref[3 * count :]
    total_ref[:features] = dot_tn(
        jnp.concatenate([node, node_below_first, node_below_second], axis=0),
        jnp.concatenate([own_ref[...].astype(BF16), grads_low], axis=0),
    )
    tops = [grads_ref[((ex - 1) * ey + y) * nz : ((ex - 1) * ey + y + 1) * nz] for y in range(ey)]
    tops += [grads_ref[count + (x * ey + ey - 1) * nz : count + (x * ey + ey) * nz] for x in range(ex)]
    total_ref[features : 2 * features] = dot_tn(
        jnp.concatenate([node, node_above_first, node_above_second], axis=0),
        jnp.concatenate([enter_ref[...].astype(BF16), *tops], axis=0),
    )
    edges = edge_ref[...].reshape(-1, features)
    total_ref[2 * features : 3 * features] = dot_tn(
        jnp.concatenate([edges, edge_below_first, edge_below_second], axis=0), grads_ref[...]
    )
    total_ref[3 * features :] = dot_tn(summed_ref[...], update_ref[...])

    if send_ref is None:
        keep_ref[...] = total_ref[...]
        return
    planes = keep_ref.shape[0]
    seconds, chunk = lax.axis_size("gy"), keep_ref.shape[1] // lax.axis_size("gy")
    edge_rows, node_rows = chunk * 3 // 4, chunk // 4
    core, plane = at_first % 2, at_first // 2
    for block in range(planes):
        for second in range(seconds):
            there = (plane ^ block) * 2
            start = second * chunk
            for flip in (core, 1 - core):
                device = (there + flip) * seconds + (at_second ^ second)
                edge = total_ref[pl.ds(pl.multiple_of(device * edge_rows, 8), edge_rows)]
                node = total_ref[pl.ds(pl.multiple_of(3 * features + device * node_rows, 8), node_rows)]
                if flip is core:
                    keep_ref[block, start : start + edge_rows] = edge
                    keep_ref[block, start + edge_rows : start + chunk] = node
                else:
                    send_at = block * seconds * chunk + start
                    send_ref[send_at : send_at + edge_rows] = edge.astype(BF16)
                    send_ref[send_at + edge_rows : send_at + chunk] = node.astype(BF16)


def node_grad_kernel(
    dims, own_ref, enter_ref, slope_top_first_ref, slope_low_first_ref, slope_top_second_ref, slope_low_second_ref,
    pair_first_ref, odd_first_ref, pair_second_ref, odd_second_ref, cotangent_ref, weight_ref, out_ref,
):
    ex, ey, nz, features = dims
    even_first, even_second = is_even("gx"), is_even("gy")
    extra = pair_first_ref.shape[0] - ey * nz

    def rows(x, y):
        return slice((x * ey + y) * nz, (x * ey + y + 1) * nz)

    def part(index):
        return slice(index * nz, (index + 1) * nz)

    own, enter = [], []
    for x in range(ex):
        for y in range(ey):
            grad = own_ref[rows(x, y)]
            pair_first = pair_first_ref[extra + y * nz : extra + (y + 1) * nz].astype(F32)
            odd_first = odd_first_ref[part(y)].astype(F32)
            pair_second, odd_second = pair_second_ref[part(x)].astype(F32), odd_second_ref[part(x)].astype(F32)
            if x == ex - 1:
                grad = grad - jnp.where(even_first, pair_first, odd_first) * slope_top_first_ref[part(y)]
            if y == ey - 1:
                grad = grad - jnp.where(even_second, pair_second, odd_second) * slope_top_second_ref[part(x)]
            own.append(grad.astype(BF16))
            grad = enter_ref[rows(x, y)]
            if x == 0:
                grad = grad + jnp.where(even_first, odd_first, pair_first) * slope_low_first_ref[part(y)]
            if y == 0:
                grad = grad + jnp.where(even_second, odd_second, pair_second) * slope_low_second_ref[part(x)]
            enter.append(grad.astype(BF16))
    result = dot_nt(jnp.concatenate(own, axis=0), weight_ref[:features])
    result = result + dot_nt(jnp.concatenate(enter, axis=0), weight_ref[features : 2 * features])
    result = result + cotangent_ref[...].reshape(-1, features).astype(F32)
    out_ref[...] = result.astype(BF16).reshape(out_ref.shape)


def pair_sum_kernel(keep_ref, received_ref, kept_ref, *send_refs):
    rows = kept_ref.shape[0]
    kept_ref[...] = keep_ref[0] + received_ref[:rows].astype(F32)
    for index, send_ref in enumerate(send_refs, 1):
        send_ref[...] = (keep_ref[index] + received_ref[index * rows : (index + 1) * rows].astype(F32)).astype(BF16)


def plane_sum_kernel(groups, keep_ref, *refs):
    received, kept_ref, send_refs = refs[: groups[0] - 1], refs[groups[0] - 1], refs[groups[0] :]
    chunk = kept_ref.shape[0]
    for index in range(groups[1]):
        here = slice(index * chunk, (index + 1) * chunk)
        total = keep_ref[here]
        for ref in received:
            total = total + ref[here].astype(F32)
        if index == 0:
            kept_ref[...] = total
        else:
            send_refs[index - 1][...] = total.astype(BF16)


def last_sum_kernel(keep_ref, *refs):
    received, edge_ref, node_ref = refs[:-2], refs[-2], refs[-1]
    total = keep_ref[...]
    for ref in received:
        total = total + ref[...].astype(F32)
    lanes = edge_ref.shape[1]
    pieces = total.shape[1] // lanes
    edge_rows, node_rows = edge_ref.shape[0] // pieces, node_ref.shape[0] // pieces
    for piece in range(pieces):
        across = slice(piece * lanes, (piece + 1) * lanes)
        edge_ref[pl.ds(piece, edge_rows, stride=pieces)] = total[:edge_rows, across]
        node_ref[pl.ds(piece, node_rows, stride=pieces)] = total[edge_rows:, across]


def local(node_features, edge_features, open_faces, edge_weight, node_weight, cotangent):
    dims = ex, ey, nz, features = node_features.shape
    firsts, seconds = lax.axis_size("gx"), lax.axis_size("gy")
    devices = firsts * seconds
    count = ex * ey * nz

    face_first, face_second = (ey * nz, features), (ex * nz, features)
    packed_first, packed_second = (2 * ey * nz + PAD, features), (2 * ex * nz + PAD, features)
    copies = 3 * (ex + ey) + 1
    pair_first, odd_first, pair_second, odd_second = call(
        functools.partial(pack_kernel, dims),
        [(packed_first, BF16)] * 2 + [(packed_second, BF16)] * 2,
        [node_features, edge_features, open_faces],
        scratch=[pltpu.VMEM(open_faces.shape, jnp.int32), pltpu.SemaphoreType.DMA((copies,))],
        far=3,
    )
    pair_second = swapped(pair_second, "gy", 0)
    odd_second = swapped(odd_second, "gy", 1)
    odd_first = swapped(odd_first, "gx", 1)
    pair_first = swapped(pair_first, "gx", 0)
    before = [((count, features), F32), ((3, count, features), F32)] + [(face_first, F32)] * 2 + [(face_second, F32)] * 2
    before = call(
        functools.partial(before_kernel, dims),
        before,
        [node_features, edge_features, edge_weight, open_faces],
        scratch=[
            pltpu.VMEM((count, features), F32),
            pltpu.VMEM((3, count, features), F32),
            pltpu.VMEM((3, count, features), F32),
            pltpu.VMEM(node_features.shape, BF16),
            pltpu.VMEM(edge_features.shape, BF16),
            pltpu.VMEM(edge_weight.shape, BF16),
            pltpu.VMEM(open_faces.shape, jnp.int32),
            pltpu.SemaphoreType.DMA((4,)),
        ],
        limit=12 << 20,
        far=4,
    )
    total_rows = 4 * features
    chunk = total_rows // devices
    by_hand = (
        total_rows % devices == 0
        and chunk % 64 == 0
        and features % 128 == 0
        and firsts % 2 == 0
        and firsts & (firsts - 1) == 0
        and seconds & (seconds - 1) == 0
    )
    planes = firsts // 2
    outs = [(node_features.shape, BF16), (face_first, BF16), (face_second, BF16), (face_second, BF16)]
    outs += [((count, features), F32)] * 2 + [(face_first, F32)] * 2 + [(face_second, F32)] * 2
    if by_hand:
        outs += [((planes * seconds * chunk + ey * nz, features), BF16), ((planes, seconds * chunk, features), F32)]

        def kernel(*refs):
            layer_kernel(dims, *refs[:26], None, *refs[26:])

    else:
        outs += [(face_first, BF16), ((total_rows, features), F32)]

        def kernel(*refs):
            layer_kernel(dims, *refs[:27], None, *refs[27:])

    low_rows = (ex + ey) * nz
    results = call(
        kernel,
        outs,
        [
            *before, edge_weight, node_weight, node_features, edge_features, open_faces, cotangent,
            pair_first, odd_first, pair_second, odd_second,
        ],
        scratch=[
            pltpu.VMEM((count, features), BF16),
            pltpu.VMEM((count, features), BF16),
            pltpu.VMEM((3, count, features), F32),
            pltpu.VMEM((low_rows, features), F32),
            pltpu.VMEM((3 * count + low_rows, features), BF16),
            pltpu.VMEM((total_rows, features), F32),
        ],
        limit=14 << 20,
    )
    new_nodes, odd_first, pair_second, odd_second = results[:4]
    received, keep = results[10:]
    received = swapped(received, "gx", 0)
    pair_second = swapped(pair_second, "gy", 0)
    odd_second = swapped(odd_second, "gy", 1)
    odd_first = swapped(odd_first, "gx", 1)
    (node_grad,) = call(
        functools.partial(node_grad_kernel, dims),
        [(node_features.shape, BF16)],
        [
            *results[4:10], received, odd_first, pair_second, odd_second, cotangent, edge_weight,
        ],
    )
    if not by_hand:
        total = keep
        edge_part = lax.psum_scatter(total[: 3 * features].reshape(-1), ("gx", "gy"), scatter_dimension=0, tiled=True)
        node_part = lax.psum_scatter(total[3 * features :].reshape(-1), ("gx", "gy"), scatter_dimension=0, tiled=True)
        return new_nodes, node_grad, edge_part, node_part

    block = (seconds * chunk, features)
    kept, *sends = call(pair_sum_kernel, [(block, F32)] + [(block, BF16)] * (planes - 1), [keep, received])
    arrived = []
    for index, value in enumerate(sends):
        arrived.append(exchanged(value, "gx", 2 * (index + 1)))
    kept, *sends = call(
        functools.partial(plane_sum_kernel, (planes, seconds)),
        [((chunk, features), F32)] + [((chunk, features), BF16)] * (seconds - 1),
        [kept, *arrived],
    )
    arrived = []
    for index, value in enumerate(sends):
        arrived.append(exchanged(value, "gy", index + 1))
    pieces = features // 128
    edge_part, node_part = call(
        last_sum_kernel, [((chunk * 3 // 4 * pieces, 128), F32), ((chunk // 4 * pieces, 128), F32)], [kept, *arrived]
    )
    return new_nodes, node_grad, edge_part.reshape(-1), node_part.reshape(-1)


def solution(mesh):
    placed = (
        P("gx", "gy", None, None),
        P(None, "gx", "gy", None, None),
        P(None, "gx", "gy", None),
        P(),
        P(),
        P("gx", "gy", None, None),
    )
    return jax.shard_map(
        local,
        mesh=mesh,
        in_specs=placed,
        out_specs=(
            P("gx", "gy", None, None),
            P("gx", "gy", None, None),
            P(("gx", "gy")),
            P(("gx", "gy")),
        ),
        check_vma=False,
    )
```

```python
import functools

import jax
import jax.numpy as jnp
from jax import lax
from jax.experimental import pallas as pl
from jax.experimental.pallas import tpu as pltpu
from jax.sharding import PartitionSpec as P

F32 = jnp.float32
BF16 = jnp.bfloat16
PAD = 16


def swapped(value, axis, first):
    count = lax.axis_size(axis)
    lower = range(first, count - 1, 2)
    return lax.ppermute(value, axis, [(at, at + 1) for at in lower] + [(at + 1, at) for at in lower])


def exchanged(value, axis, flip):
    count = lax.axis_size(axis)
    return lax.ppermute(value, axis, [(source, source ^ flip) for source in range(count)])


def dot(left, right):
    return jnp.dot(left, right, preferred_element_type=F32)


def dot_nt(left, right):
    return lax.dot_general(left, right, (((1,), (1,)), ((), ())), preferred_element_type=F32)


def dot_tn(left, right):
    return lax.dot_general(left, right, (((0,), (0,)), ((), ())), preferred_element_type=F32)


def column_of(row):
    size = row.shape[-1]
    spread = jnp.broadcast_to(row, (size, size))
    down = lax.broadcasted_iota(jnp.int32, (size, size), 0)
    across = lax.broadcasted_iota(jnp.int32, (size, size), 1)
    return jnp.sum(jnp.where(down == across, spread, 0.0), axis=1, keepdims=True)


def sigmoid(values):
    return 0.5 * jnp.tanh(0.5 * values) + 0.5


def call(kernel, outs, args, scratch=(), limit=4 << 20, cost=None, far=0):
    args = [pltpu.with_memory_space_constraint(arg, pltpu.HBM) for arg in args[:far]] + list(args[far:])
    return pl.pallas_call(
        kernel,
        out_shape=[jax.ShapeDtypeStruct(shape, dtype) for shape, dtype in outs],
        in_specs=[pl.BlockSpec(memory_space=pltpu.HBM)] * far + [pl.BlockSpec(memory_space=pltpu.VMEM)] * (len(args) - far),
        out_specs=[pl.BlockSpec(memory_space=pltpu.VMEM)] * len(outs),
        scratch_shapes=list(scratch),
        compiler_params=pltpu.CompilerParams(vmem_limit_bytes=limit),
        cost_estimate=cost,
    )(*args)


def spread_rows(rows, count):
    down = lax.broadcasted_iota(jnp.int32, (count, rows[0].shape[-1]), 0)
    tile = jnp.zeros((count, rows[0].shape[-1]), F32)
    for index, row in enumerate(rows):
        tile = jnp.where(down == index, row, tile)
    return tile


def is_even(axis):
    return lax.axis_index(axis) % 2 == 0


def pack_kernel(
    dims, node_ref, edge_ref, faces_ref, pair_first_ref, odd_first_ref, pair_second_ref, odd_second_ref, open_ref, sems
):
    ex, ey, nz, _ = dims
    faces_copy = pltpu.make_async_copy(faces_ref, open_ref, sems.at[0])
    faces_copy.start()

    def upward(ref, direction, cells):
        pairs = []
        for index, (x, y) in enumerate(cells):
            pairs.append((node_ref.at[x, y], ref.at[pl.ds(index * nz, nz)]))
            pairs.append((edge_ref.at[direction, x, y], ref.at[pl.ds((len(cells) + index) * nz, nz)]))
        return pairs

    def downward(ref, cells):
        return [(node_ref.at[x, y], ref.at[pl.ds(index * nz, nz)]) for index, (x, y) in enumerate(cells)]

    plans, used = [], 1
    for direction, axis, pair_ref, odd_ref, top, low in (
        (1, "gy", pair_second_ref, odd_second_ref, [(x, ey - 1) for x in range(ex)], [(x, 0) for x in range(ex)]),
        (0, "gx", pair_first_ref, odd_first_ref, [(ex - 1, y) for y in range(ey)], [(0, y) for y in range(ey)]),
    ):
        choices = [upward(up, direction, top) + downward(down, low) for up, down in ((pair_ref, odd_ref), (odd_ref, pair_ref))]
        copies = [
            [pltpu.make_async_copy(source, target, sems.at[used + index]) for index, (source, target) in enumerate(pairs)]
            for pairs in choices
        ]
        used += len(copies[0])
        plans.append((is_even(axis), copies, (pair_ref, odd_ref), 2 * len(top) * nz, (direction, top)))
    for even, copies, _, _, _ in plans:
        for wanted, group in ((even, copies[0]), (jnp.logical_not(even), copies[1])):
            @pl.when(wanted)
            def _():
                for copy in group:
                    copy.start()
    faces_copy.wait()
    for even, copies, refs, start, (direction, top) in plans:
        mask = spread_rows([open_ref[direction, x, y : y + 1].astype(F32) for x, y in top], PAD).astype(BF16)
        for ref in refs:
            ref[start:, :nz] = mask
        for wanted, group in ((even, copies[0]), (jnp.logical_not(even), copies[1])):
            @pl.when(wanted)
            def _():
                for copy in group:
                    copy.wait()


def edge_terms(preact, open_column):
    gate = sigmoid(preact)
    opened = gate * open_column
    message = (preact * opened).astype(BF16).astype(F32)
    return message, opened * (1.0 + preact * (1.0 - gate))


def halves(even, pair_ref, odd_ref, rows):
    def pick(first, second, start, stop):
        return jnp.where(even, first[start:stop], second[start:stop])

    return (
        pick(pair_ref, odd_ref, 0, rows),
        pick(odd_ref, pair_ref, 0, rows),
        pick(odd_ref, pair_ref, rows, 2 * rows),
        pick(odd_ref, pair_ref, 2 * rows, 2 * rows + PAD).astype(F32),
    )


def before_kernel(
    dims, node_ref, edge_ref, weight_ref, faces_ref,
    sum_ref, slope_ref, stored_top_first_ref, other_low_first_ref, stored_top_second_ref, other_low_second_ref,
    other_ref, stored_ref, message_ref, node_here, edge_here, weight_here, open_ref, sems,
):
    ex, ey, nz, features = dims
    copies = [
        pltpu.make_async_copy(node_ref, node_here, sems.at[0]),
        pltpu.make_async_copy(weight_ref, weight_here, sems.at[1]),
        pltpu.make_async_copy(edge_ref, edge_here, sems.at[2]),
        pltpu.make_async_copy(faces_ref, open_ref, sems.at[3]),
    ]
    for copy in copies:
        copy.start()

    def rows(x, y):
        return slice((x * ey + y) * nz, (x * ey + y + 1) * nz)

    def part(index):
        return slice(index * nz, (index + 1) * nz)

    copies[0].wait()
    copies[1].wait()
    node = node_here[...].reshape(-1, features)
    own = dot(node, weight_here[:features])
    other_ref[...] = dot(node, weight_here[features : 2 * features])
    copies[2].wait()
    copies[3].wait()
    for direction in range(3):
        stored_ref[direction] = own + dot(edge_here[direction].reshape(-1, features), weight_here[2 * features :])
    inside_third = jnp.where(lax.broadcasted_iota(jnp.int32, (nz, 1), 0) < nz - 1, 1.0, 0.0)
    for y in range(ey):
        stored_top_first_ref[part(y)] = stored_ref[0, rows(ex - 1, y)]
        other_low_first_ref[part(y)] = other_ref[rows(0, y)]
    for x in range(ex):
        stored_top_second_ref[part(x)] = stored_ref[1, rows(x, ey - 1)]
        other_low_second_ref[part(x)] = other_ref[rows(x, 0)]
        for y in range(ey):
            here = rows(x, y)
            column = [column_of(open_ref[direction, x, y : y + 1].astype(F32)) for direction in range(3)]
            if x + 1 < ex:
                beyond = other_ref[rows(x + 1, y)]
                message_ref[0, here], slope_ref[0, here] = edge_terms(stored_ref[0, here] + beyond, column[0])
            if y + 1 < ey:
                beyond = other_ref[rows(x, y + 1)]
                message_ref[1, here], slope_ref[1, here] = edge_terms(stored_ref[1, here] + beyond, column[1])
            beyond = pltpu.roll(other_ref[here], nz - 1, 0)
            message_ref[2, here], slope_ref[2, here] = edge_terms(stored_ref[2, here] + beyond, column[2] * inside_third)
    for x in range(ex):
        for y in range(ey):
            here = rows(x, y)
            third = message_ref[2, here]
            total = third - pltpu.roll(third, 1, 0)
            if x + 1 < ex:
                total = total + message_ref[0, here]
            if x > 0:
                total = total - message_ref[0, rows(x - 1, y)]
            if y + 1 < ey:
                total = total + message_ref[1, here]
            if y > 0:
                total = total - message_ref[1, rows(x, y - 1)]
            sum_ref[here] = total


def layer_kernel(
    dims,
    sum_ref, slope_ref, stored_top_first_ref, other_low_first_ref, stored_top_second_ref, other_low_second_ref,
    weight_ref, node_weight_ref, node_ref, edge_ref, open_ref, cotangent_ref,
    pair_first_ref, odd_first_ref, pair_second_ref, odd_second_ref,
    new_ref, grad_odd_first_ref, grad_pair_second_ref, grad_odd_second_ref,
    own_ref, enter_ref, slope_top_first_ref, slope_low_first_ref, slope_top_second_ref, slope_low_second_ref,
    grad_pair_first_ref, send_ref, keep_ref,
    summed_ref, update_ref, grad_ref, grad_low_ref, grads_ref, total_ref,
):
    ex, ey, nz, features = dims
    at_first, at_second = lax.axis_index("gx"), lax.axis_index("gy")
    inside_first = (at_first < lax.axis_size("gx") - 1).astype(F32)
    inside_second = (at_second < lax.axis_size("gy") - 1).astype(F32)
    even_first, even_second = is_even("gx"), is_even("gy")

    def rows(x, y):
        return slice((x * ey + y) * nz, (x * ey + y + 1) * nz)

    def part(index):
        return slice(index * nz, (index + 1) * nz)

    rows_first, rows_second = ey * nz, ex * nz
    node_above_first, node_below_first, edge_below_first, mask_first = halves(
        even_first, pair_first_ref, odd_first_ref, rows_first
    )
    node_above_second, node_below_second, edge_below_second, mask_second = halves(
        even_second, pair_second_ref, odd_second_ref, rows_second
    )
    other_weight = weight_ref[features : 2 * features]
    above_first, above_second = dot(node_above_first, other_weight), dot(node_above_second, other_weight)
    entering_first = dot(node_below_first, weight_ref[:features]) + dot(edge_below_first, weight_ref[2 * features :])
    entering_second = dot(node_below_second, weight_ref[:features]) + dot(edge_below_second, weight_ref[2 * features :])
    totals = [[sum_ref[rows(x, y)] for y in range(ey)] for x in range(ex)]
    for y in range(ey):
        here = part(y)
        column = column_of(open_ref[0, ex - 1, y : y + 1].astype(F32)) * inside_first
        message, slope_top_first_ref[here] = edge_terms(stored_top_first_ref[here] + above_first[here], column)
        totals[ex - 1][y] = totals[ex - 1][y] + message
        column = column_of(mask_first[y : y + 1, :nz])
        message, slope_low_first_ref[here] = edge_terms(entering_first[here] + other_low_first_ref[here], column)
        totals[0][y] = totals[0][y] - message
    for x in range(ex):
        here = part(x)
        column = column_of(open_ref[1, x, ey - 1 : ey].astype(F32)) * inside_second
        message, slope_top_second_ref[here] = edge_terms(stored_top_second_ref[here] + above_second[here], column)
        totals[x][ey - 1] = totals[x][ey - 1] + message
        column = column_of(mask_second[x : x + 1, :nz])
        message, slope_low_second_ref[here] = edge_terms(entering_second[here] + other_low_second_ref[here], column)
        totals[x][0] = totals[x][0] - message
    for x in range(ex):
        for y in range(ey):
            summed_ref[rows(x, y)] = totals[x][y].astype(BF16)

    node = node_ref[...].reshape(-1, features)
    update = dot(summed_ref[...], node_weight_ref[...])
    gate = sigmoid(update)
    new_ref[...] = (node.astype(F32) + update * gate).astype(BF16).reshape(new_ref.shape)
    cotangent = cotangent_ref[...].reshape(-1, features).astype(F32)
    update_ref[...] = (cotangent * (gate * (1.0 + update * (1.0 - gate)))).astype(BF16)
    grad_summed = dot_nt(update_ref[...], node_weight_ref[...]).astype(BF16)
    pair_target, extra = (grad_pair_first_ref, 0) if send_ref is None else (send_ref, send_ref.shape[0] - rows_first)
    for y in range(ey):
        low, top = grad_summed[rows(0, y)], grad_summed[rows(ex - 1, y)]
        pair_target[extra + y * nz : extra + (y + 1) * nz] = jnp.where(even_first, top, low)
        grad_odd_first_ref[part(y)] = jnp.where(even_first, low, top)
    for x in range(ex):
        low, top = grad_summed[rows(x, 0)], grad_summed[rows(x, ey - 1)]
        grad_pair_second_ref[part(x)] = jnp.where(even_second, top, low)
        grad_odd_second_ref[part(x)] = jnp.where(even_second, low, top)
    wide = grad_summed.astype(F32)

    count = ex * ey * nz
    for index in range(ey + ex):
        cell = rows(0, index) if index < ey else rows(index - ey, 0)
        slope = slope_low_first_ref[part(index)] if index < ey else slope_low_second_ref[part(index - ey)]
        grad = -wide[cell] * slope
        grad_low_ref[part(index)] = grad
        grads_ref[3 * count + index * nz : 3 * count + (index + 1) * nz] = grad.astype(BF16)
    for x in range(ex):
        for y in range(ey):
            here = rows(x, y)
            mine = wide[here]
            lead = [
                mine - wide[rows(x + 1, y)] if x + 1 < ex else mine,
                mine - wide[rows(x, y + 1)] if y + 1 < ey else mine,
                mine - pltpu.roll(mine, nz - 1, 0),
            ]
            for direction in range(3):
                if direction == 0 and x == ex - 1:
                    slope = slope_top_first_ref[part(y)]
                elif direction == 1 and y == ey - 1:
                    slope = slope_top_second_ref[part(x)]
                else:
                    slope = slope_ref[direction, here]
                grad = lead[direction] * slope
                grad_ref[direction, here] = grad
                start = direction * count + (x * ey + y) * nz
                grads_ref[start : start + nz] = grad.astype(BF16)
    for x in range(ex):
        for y in range(ey):
            here = rows(x, y)
            third = grad_ref[2, here]
            own_ref[here] = grad_ref[0, here] + grad_ref[1, here] + third
            enter = pltpu.roll(third, 1, 0)
            enter = enter + (grad_ref[0, rows(x - 1, y)] if x > 0 else grad_low_ref[part(y)])
            enter = enter + (grad_ref[1, rows(x, y - 1)] if y > 0 else grad_low_ref[part(ey + x)])
            enter_ref[here] = enter

    grads_low = grads_ref[3 * count :]
    total_ref[:features] = dot_tn(
        jnp.concatenate([node, node_below_first, node_below_second], axis=0),
        jnp.concatenate([own_ref[...].astype(BF16), grads_low], axis=0),
    )
    tops = [grads_ref[((ex - 1) * ey + y) * nz : ((ex - 1) * ey + y + 1) * nz] for y in range(ey)]
    tops += [grads_ref[count + (x * ey + ey - 1) * nz : count + (x * ey + ey) * nz] for x in range(ex)]
    total_ref[features : 2 * features] = dot_tn(
        jnp.concatenate([node, node_above_first, node_above_second], axis=0),
        jnp.concatenate([enter_ref[...].astype(BF16), *tops], axis=0),
    )
    edges = edge_ref[...].reshape(-1, features)
    total_ref[2 * features : 3 * features] = dot_tn(
        jnp.concatenate([edges, edge_below_first, edge_below_second], axis=0), grads_ref[...]
    )
    total_ref[3 * features :] = dot_tn(summed_ref[...], update_ref[...])

    if send_ref is None:
        keep_ref[...] = total_ref[...]
        return
    planes = keep_ref.shape[0]
    seconds, chunk = lax.axis_size("gy"), keep_ref.shape[1] // lax.axis_size("gy")
    edge_rows, node_rows = chunk * 3 // 4, chunk // 4
    core, plane = at_first % 2, at_first // 2
    for block in range(planes):
        for second in range(seconds):
            there = (plane ^ block) * 2
            start = second * chunk
            for flip in (core, 1 - core):
                device = (there + flip) * seconds + (at_second ^ second)
                edge = total_ref[pl.ds(pl.multiple_of(device * edge_rows, 8), edge_rows)]
                node = total_ref[pl.ds(pl.multiple_of(3 * features + device * node_rows, 8), node_rows)]
                if flip is core:
                    keep_ref[block, start : start + edge_rows] = edge
                    keep_ref[block, start + edge_rows : start + chunk] = node
                else:
                    send_at = block * seconds * chunk + start
                    send_ref[send_at : send_at + edge_rows] = edge.astype(BF16)
                    send_ref[send_at + edge_rows : send_at + chunk] = node.astype(BF16)


def node_grad_kernel(
    dims, own_ref, enter_ref, slope_top_first_ref, slope_low_first_ref, slope_top_second_ref, slope_low_second_ref,
    pair_first_ref, odd_first_ref, pair_second_ref, odd_second_ref, cotangent_ref, weight_ref, out_ref,
):
    ex, ey, nz, features = dims
    even_first, even_second = is_even("gx"), is_even("gy")
    extra = pair_first_ref.shape[0] - ey * nz

    def rows(x, y):
        return slice((x * ey + y) * nz, (x * ey + y + 1) * nz)

    def part(index):
        return slice(index * nz, (index + 1) * nz)

    own, enter = [], []
    for x in range(ex):
        for y in range(ey):
            grad = own_ref[rows(x, y)]
            pair_first = pair_first_ref[extra + y * nz : extra + (y + 1) * nz].astype(F32)
            odd_first = odd_first_ref[part(y)].astype(F32)
            pair_second, odd_second = pair_second_ref[part(x)].astype(F32), odd_second_ref[part(x)].astype(F32)
            if x == ex - 1:
                grad = grad - jnp.where(even_first, pair_first, odd_first) * slope_top_first_ref[part(y)]
            if y == ey - 1:
                grad = grad - jnp.where(even_second, pair_second, odd_second) * slope_top_second_ref[part(x)]
            own.append(grad.astype(BF16))
            grad = enter_ref[rows(x, y)]
            if x == 0:
                grad = grad + jnp.where(even_first, odd_first, pair_first) * slope_low_first_ref[part(y)]
            if y == 0:
                grad = grad + jnp.where(even_second, odd_second, pair_second) * slope_low_second_ref[part(x)]
            enter.append(grad.astype(BF16))
    result = dot_nt(jnp.concatenate(own, axis=0), weight_ref[:features])
    result = result + dot_nt(jnp.concatenate(enter, axis=0), weight_ref[features : 2 * features])
    result = result + cotangent_ref[...].reshape(-1, features).astype(F32)
    out_ref[...] = result.astype(BF16).reshape(out_ref.shape)


def pair_sum_kernel(keep_ref, received_ref, near_kept_ref, far_kept_ref, *send_refs):
    near, far = near_kept_ref.shape[0], far_kept_ref.shape[0]
    planes = len(send_refs) // 2 + 1
    for plane in range(planes):
        start = plane * (near + far)
        for first, size, kept_ref, sends in (
            (near, far, far_kept_ref, send_refs[: planes - 1]),
            (0, near, near_kept_ref, send_refs[planes - 1 :]),
        ):
            total = keep_ref[plane, first : first + size] + received_ref[start + first : start + first + size].astype(F32)
            if plane == 0:
                kept_ref[...] = total
            else:
                sends[plane - 1][...] = total.astype(BF16)


def plane_sum_kernel(received, *refs):
    kept_ref, arrived, outs = refs[0], refs[1 : received + 1], refs[received + 1 :]
    chunk = outs[0].shape[0]
    for index, out in enumerate(outs):
        here = slice(index * chunk, (index + 1) * chunk)
        total = kept_ref[here]
        for ref in arrived:
            total = total + ref[here].astype(F32)
        out[...] = total.astype(out.dtype)


def last_sum_kernel(keep_ref, *refs):
    received, edge_ref, node_ref = refs[:-2], refs[-2], refs[-1]
    total = keep_ref[...]
    for ref in received:
        total = total + ref[...].astype(F32)
    lanes = edge_ref.shape[1]
    pieces = total.shape[1] // lanes
    edge_rows, node_rows = edge_ref.shape[0] // pieces, node_ref.shape[0] // pieces
    for piece in range(pieces):
        across = slice(piece * lanes, (piece + 1) * lanes)
        edge_ref[pl.ds(piece, edge_rows, stride=pieces)] = total[:edge_rows, across]
        node_ref[pl.ds(piece, node_rows, stride=pieces)] = total[edge_rows:, across]


def local(node_features, edge_features, open_faces, edge_weight, node_weight, cotangent):
    dims = ex, ey, nz, features = node_features.shape
    firsts, seconds = lax.axis_size("gx"), lax.axis_size("gy")
    devices = firsts * seconds
    count = ex * ey * nz

    face_first, face_second = (ey * nz, features), (ex * nz, features)
    packed_first, packed_second = (2 * ey * nz + PAD, features), (2 * ex * nz + PAD, features)
    copies = 3 * (ex + ey) + 1
    pair_first, odd_first, pair_second, odd_second = call(
        functools.partial(pack_kernel, dims),
        [(packed_first, BF16)] * 2 + [(packed_second, BF16)] * 2,
        [node_features, edge_features, open_faces],
        scratch=[pltpu.VMEM(open_faces.shape, jnp.int32), pltpu.SemaphoreType.DMA((copies,))],
        far=3,
    )
    pair_second = swapped(pair_second, "gy", 0)
    odd_second = swapped(odd_second, "gy", 1)
    odd_first = swapped(odd_first, "gx", 1)
    pair_first = swapped(pair_first, "gx", 0)
    before = [((count, features), F32), ((3, count, features), F32)] + [(face_first, F32)] * 2 + [(face_second, F32)] * 2
    before = call(
        functools.partial(before_kernel, dims),
        before,
        [node_features, edge_features, edge_weight, open_faces],
        scratch=[
            pltpu.VMEM((count, features), F32),
            pltpu.VMEM((3, count, features), F32),
            pltpu.VMEM((3, count, features), F32),
            pltpu.VMEM(node_features.shape, BF16),
            pltpu.VMEM(edge_features.shape, BF16),
            pltpu.VMEM(edge_weight.shape, BF16),
            pltpu.VMEM(open_faces.shape, jnp.int32),
            pltpu.SemaphoreType.DMA((4,)),
        ],
        limit=12 << 20,
        far=4,
    )
    total_rows = 4 * features
    chunk = total_rows // devices
    by_hand = (
        total_rows % devices == 0
        and chunk % 64 == 0
        and features % 128 == 0
        and firsts % 2 == 0
        and firsts & (firsts - 1) == 0
        and seconds & (seconds - 1) == 0
        and seconds > 1
    )
    planes = firsts // 2
    outs = [(node_features.shape, BF16), (face_first, BF16), (face_second, BF16), (face_second, BF16)]
    outs += [((count, features), F32)] * 2 + [(face_first, F32)] * 2 + [(face_second, F32)] * 2
    if by_hand:
        outs += [((planes * seconds * chunk + ey * nz, features), BF16), ((planes, seconds * chunk, features), F32)]

        def kernel(*refs):
            layer_kernel(dims, *refs[:26], None, *refs[26:])

    else:
        outs += [(face_first, BF16), ((total_rows, features), F32)]

        def kernel(*refs):
            layer_kernel(dims, *refs[:27], None, *refs[27:])

    low_rows = (ex + ey) * nz
    results = call(
        kernel,
        outs,
        [
            *before, edge_weight, node_weight, node_features, edge_features, open_faces, cotangent,
            pair_first, odd_first, pair_second, odd_second,
        ],
        scratch=[
            pltpu.VMEM((count, features), BF16),
            pltpu.VMEM((count, features), BF16),
            pltpu.VMEM((3, count, features), F32),
            pltpu.VMEM((low_rows, features), F32),
            pltpu.VMEM((3 * count + low_rows, features), BF16),
            pltpu.VMEM((total_rows, features), F32),
        ],
        limit=14 << 20,
    )
    new_nodes, odd_first, pair_second, odd_second = results[:4]
    received, keep = results[10:]
    received = swapped(received, "gx", 0)
    pair_second = swapped(pair_second, "gy", 0)
    odd_second = swapped(odd_second, "gy", 1)
    odd_first = swapped(odd_first, "gx", 1)
    (node_grad,) = call(
        functools.partial(node_grad_kernel, dims),
        [(node_features.shape, BF16)],
        [
            *results[4:10], received, odd_first, pair_second, odd_second, cotangent, edge_weight,
        ],
    )
    if not by_hand:
        total = keep
        edge_part = lax.psum_scatter(total[: 3 * features].reshape(-1), ("gx", "gy"), scatter_dimension=0, tiled=True)
        node_part = lax.psum_scatter(total[3 * features :].reshape(-1), ("gx", "gy"), scatter_dimension=0, tiled=True)
        return new_nodes, node_grad, edge_part, node_part

    near, far = (seconds // 2 * chunk, features), ((seconds - seconds // 2) * chunk, features)
    near_kept, far_kept, *sends = call(
        pair_sum_kernel, [(near, F32), (far, F32)] + [(far, BF16)] * (planes - 1) + [(near, BF16)] * (planes - 1), [keep, received]
    )

    def over_planes(values):
        arrived = []
        for index, value in enumerate(values):
            arrived.append(exchanged(value, "gx", 2 * (index + 1)))
        return arrived

    far_arrived, near_arrived = over_planes(sends[: planes - 1]), over_planes(sends[planes - 1 :])
    piece = ((chunk, features), BF16)
    far_sends = call(
        functools.partial(plane_sum_kernel, planes - 1), [piece] * (seconds - seconds // 2), [far_kept, *far_arrived]
    )
    kept, *near_sends = call(
        functools.partial(plane_sum_kernel, planes - 1),
        [((chunk, features), F32)] + [piece] * (seconds // 2 - 1),
        [near_kept, *near_arrived],
    )
    arrived = []
    for index, value in enumerate([*near_sends, *far_sends]):
        arrived.append(exchanged(value, "gy", index + 1))
    pieces = features // 128
    edge_part, node_part = call(
        last_sum_kernel, [((chunk * 3 // 4 * pieces, 128), F32), ((chunk // 4 * pieces, 128), F32)], [kept, *arrived]
    )
    return new_nodes, node_grad, edge_part.reshape(-1), node_part.reshape(-1)


def solution(mesh):
    placed = (
        P("gx", "gy", None, None),
        P(None, "gx", "gy", None, None),
        P(None, "gx", "gy", None),
        P(),
        P(),
        P("gx", "gy", None, None),
    )
    return jax.shard_map(
        local,
        mesh=mesh,
        in_specs=placed,
        out_specs=(
            P("gx", "gy", None, None),
            P("gx", "gy", None, None),
            P(("gx", "gy")),
            P(("gx", "gy")),
        ),
        check_vma=False,
    )
```

```python
import functools

import jax
import jax.numpy as jnp
from jax import lax
from jax.experimental import pallas as pl
from jax.experimental.pallas import tpu as pltpu
from jax.sharding import PartitionSpec as P

F32 = jnp.float32
BF16 = jnp.bfloat16
PAD = 16


def swapped(value, axis, first):
    count = lax.axis_size(axis)
    lower = range(first, count - 1, 2)
    return lax.ppermute(value, axis, [(at, at + 1) for at in lower] + [(at + 1, at) for at in lower])


def exchanged(value, axis, flip):
    count = lax.axis_size(axis)
    return lax.ppermute(value, axis, [(source, source ^ flip) for source in range(count)])


def dot(left, right):
    return jnp.dot(left, right, preferred_element_type=F32)


def dot_nt(left, right):
    return lax.dot_general(left, right, (((1,), (1,)), ((), ())), preferred_element_type=F32)


def dot_tn(left, right):
    return lax.dot_general(left, right, (((0,), (0,)), ((), ())), preferred_element_type=F32)


def column_of(row):
    size = row.shape[-1]
    spread = jnp.broadcast_to(row, (size, size))
    down = lax.broadcasted_iota(jnp.int32, (size, size), 0)
    across = lax.broadcasted_iota(jnp.int32, (size, size), 1)
    return jnp.sum(jnp.where(down == across, spread, 0.0), axis=1, keepdims=True)


def sigmoid(values):
    return 0.5 * jnp.tanh(0.5 * values) + 0.5


def call(kernel, outs, args, scratch=(), limit=4 << 20, cost=None, far=0):
    args = [pltpu.with_memory_space_constraint(arg, pltpu.HBM) for arg in args[:far]] + list(args[far:])
    return pl.pallas_call(
        kernel,
        out_shape=[jax.ShapeDtypeStruct(shape, dtype) for shape, dtype in outs],
        in_specs=[pl.BlockSpec(memory_space=pltpu.HBM)] * far + [pl.BlockSpec(memory_space=pltpu.VMEM)] * (len(args) - far),
        out_specs=[pl.BlockSpec(memory_space=pltpu.VMEM)] * len(outs),
        scratch_shapes=list(scratch),
        compiler_params=pltpu.CompilerParams(vmem_limit_bytes=limit),
        cost_estimate=cost,
    )(*args)


def spread_rows(rows, count):
    down = lax.broadcasted_iota(jnp.int32, (count, rows[0].shape[-1]), 0)
    tile = jnp.zeros((count, rows[0].shape[-1]), F32)
    for index, row in enumerate(rows):
        tile = jnp.where(down == index, row, tile)
    return tile


def is_even(axis):
    return lax.axis_index(axis) % 2 == 0


def pack_kernel(
    dims, node_ref, edge_ref, faces_ref, pair_first_ref, odd_first_ref, pair_second_ref, odd_second_ref, open_ref, sems
):
    ex, ey, nz, _ = dims
    faces_copy = pltpu.make_async_copy(faces_ref, open_ref, sems.at[0])
    faces_copy.start()

    def upward(ref, direction, cells):
        pairs = []
        for index, (x, y) in enumerate(cells):
            pairs.append((node_ref.at[x, y], ref.at[pl.ds(index * nz, nz)]))
            pairs.append((edge_ref.at[direction, x, y], ref.at[pl.ds((len(cells) + index) * nz, nz)]))
        return pairs

    def downward(ref, cells):
        return [(node_ref.at[x, y], ref.at[pl.ds(index * nz, nz)]) for index, (x, y) in enumerate(cells)]

    plans, used = [], 1
    for direction, axis, pair_ref, odd_ref, top, low in (
        (1, "gy", pair_second_ref, odd_second_ref, [(x, ey - 1) for x in range(ex)], [(x, 0) for x in range(ex)]),
        (0, "gx", pair_first_ref, odd_first_ref, [(ex - 1, y) for y in range(ey)], [(0, y) for y in range(ey)]),
    ):
        choices = [upward(up, direction, top) + downward(down, low) for up, down in ((pair_ref, odd_ref), (odd_ref, pair_ref))]
        copies = [
            [pltpu.make_async_copy(source, target, sems.at[used + index]) for index, (source, target) in enumerate(pairs)]
            for pairs in choices
        ]
        used += len(copies[0])
        plans.append((is_even(axis), copies, (pair_ref, odd_ref), 2 * len(top) * nz, (direction, top)))
    for even, copies, _, _, _ in plans:
        for wanted, group in ((even, copies[0]), (jnp.logical_not(even), copies[1])):
            @pl.when(wanted)
            def _():
                for copy in group:
                    copy.start()
    faces_copy.wait()
    for even, copies, refs, start, (direction, top) in plans:
        mask = spread_rows([open_ref[direction, x, y : y + 1].astype(F32) for x, y in top], PAD).astype(BF16)
        for ref in refs:
            ref[start:, :nz] = mask
        for wanted, group in ((even, copies[0]), (jnp.logical_not(even), copies[1])):
            @pl.when(wanted)
            def _():
                for copy in group:
                    copy.wait()


def edge_terms(preact, open_column):
    gate = sigmoid(preact)
    opened = gate * open_column
    message = (preact * opened).astype(BF16).astype(F32)
    return message, opened * (1.0 + preact * (1.0 - gate))


def halves(even, pair_ref, odd_ref, rows):
    def pick(first, second, start, stop):
        return jnp.where(even, first[start:stop], second[start:stop])

    return (
        pick(pair_ref, odd_ref, 0, rows),
        pick(odd_ref, pair_ref, 0, rows),
        pick(odd_ref, pair_ref, rows, 2 * rows),
        pick(odd_ref, pair_ref, 2 * rows, 2 * rows + PAD).astype(F32),
    )


def before_kernel(
    dims, node_ref, edge_ref, weight_ref, faces_ref,
    sum_ref, slope_ref, stored_top_first_ref, other_low_first_ref, stored_top_second_ref, other_low_second_ref,
    other_ref, stored_ref, message_ref, node_here, edge_here, weight_here, open_ref, sems,
):
    ex, ey, nz, features = dims
    copies = [
        pltpu.make_async_copy(node_ref, node_here, sems.at[0]),
        pltpu.make_async_copy(weight_ref, weight_here, sems.at[1]),
        pltpu.make_async_copy(edge_ref, edge_here, sems.at[2]),
        pltpu.make_async_copy(faces_ref, open_ref, sems.at[3]),
    ]
    for copy in copies:
        copy.start()

    def rows(x, y):
        return slice((x * ey + y) * nz, (x * ey + y + 1) * nz)

    def part(index):
        return slice(index * nz, (index + 1) * nz)

    copies[0].wait()
    copies[1].wait()
    node = node_here[...].reshape(-1, features)
    own = dot(node, weight_here[:features])
    other_ref[...] = dot(node, weight_here[features : 2 * features])
    copies[2].wait()
    copies[3].wait()
    for direction in range(3):
        stored_ref[direction] = own + dot(edge_here[direction].reshape(-1, features), weight_here[2 * features :])
    inside_third = jnp.where(lax.broadcasted_iota(jnp.int32, (nz, 1), 0) < nz - 1, 1.0, 0.0)
    for y in range(ey):
        stored_top_first_ref[part(y)] = stored_ref[0, rows(ex - 1, y)]
        other_low_first_ref[part(y)] = other_ref[rows(0, y)]
    for x in range(ex):
        stored_top_second_ref[part(x)] = stored_ref[1, rows(x, ey - 1)]
        other_low_second_ref[part(x)] = other_ref[rows(x, 0)]
        for y in range(ey):
            here = rows(x, y)
            column = [column_of(open_ref[direction, x, y : y + 1].astype(F32)) for direction in range(3)]
            if x + 1 < ex:
                beyond = other_ref[rows(x + 1, y)]
                message_ref[0, here], slope_ref[0, here] = edge_terms(stored_ref[0, here] + beyond, column[0])
            if y + 1 < ey:
                beyond = other_ref[rows(x, y + 1)]
                message_ref[1, here], slope_ref[1, here] = edge_terms(stored_ref[1, here] + beyond, column[1])
            beyond = pltpu.roll(other_ref[here], nz - 1, 0)
            message_ref[2, here], slope_ref[2, here] = edge_terms(stored_ref[2, here] + beyond, column[2] * inside_third)
    for x in range(ex):
        for y in range(ey):
            here = rows(x, y)
            third = message_ref[2, here]
            total = third - pltpu.roll(third, 1, 0)
            if x + 1 < ex:
                total = total + message_ref[0, here]
            if x > 0:
                total = total - message_ref[0, rows(x - 1, y)]
            if y + 1 < ey:
                total = total + message_ref[1, here]
            if y > 0:
                total = total - message_ref[1, rows(x, y - 1)]
            sum_ref[here] = total


def layer_kernel(
    dims,
    sum_ref, slope_ref, stored_top_first_ref, other_low_first_ref, stored_top_second_ref, other_low_second_ref,
    weight_ref, node_weight_ref, node_ref, edge_ref, open_ref, cotangent_ref,
    pair_first_ref, odd_first_ref, pair_second_ref, odd_second_ref,
    new_ref, grad_odd_first_ref, grad_pair_second_ref, grad_odd_second_ref,
    own_ref, enter_ref, slope_top_first_ref, slope_low_first_ref, slope_top_second_ref, slope_low_second_ref,
    grad_pair_first_ref, far_send_ref, near_send_ref, keep_ref,
    summed_ref, update_ref, grad_ref, grad_low_ref, grads_ref, total_ref,
):
    ex, ey, nz, features = dims
    at_first, at_second = lax.axis_index("gx"), lax.axis_index("gy")
    inside_first = (at_first < lax.axis_size("gx") - 1).astype(F32)
    inside_second = (at_second < lax.axis_size("gy") - 1).astype(F32)
    even_first, even_second = is_even("gx"), is_even("gy")

    def rows(x, y):
        return slice((x * ey + y) * nz, (x * ey + y + 1) * nz)

    def part(index):
        return slice(index * nz, (index + 1) * nz)

    rows_first, rows_second = ey * nz, ex * nz
    node_above_first, node_below_first, edge_below_first, mask_first = halves(
        even_first, pair_first_ref, odd_first_ref, rows_first
    )
    node_above_second, node_below_second, edge_below_second, mask_second = halves(
        even_second, pair_second_ref, odd_second_ref, rows_second
    )
    other_weight = weight_ref[features : 2 * features]
    above_first, above_second = dot(node_above_first, other_weight), dot(node_above_second, other_weight)
    entering_first = dot(node_below_first, weight_ref[:features]) + dot(edge_below_first, weight_ref[2 * features :])
    entering_second = dot(node_below_second, weight_ref[:features]) + dot(edge_below_second, weight_ref[2 * features :])
    totals = [[sum_ref[rows(x, y)] for y in range(ey)] for x in range(ex)]
    for y in range(ey):
        here = part(y)
        column = column_of(open_ref[0, ex - 1, y : y + 1].astype(F32)) * inside_first
        message, slope_top_first_ref[here] = edge_terms(stored_top_first_ref[here] + above_first[here], column)
        totals[ex - 1][y] = totals[ex - 1][y] + message
        column = column_of(mask_first[y : y + 1, :nz])
        message, slope_low_first_ref[here] = edge_terms(entering_first[here] + other_low_first_ref[here], column)
        totals[0][y] = totals[0][y] - message
    for x in range(ex):
        here = part(x)
        column = column_of(open_ref[1, x, ey - 1 : ey].astype(F32)) * inside_second
        message, slope_top_second_ref[here] = edge_terms(stored_top_second_ref[here] + above_second[here], column)
        totals[x][ey - 1] = totals[x][ey - 1] + message
        column = column_of(mask_second[x : x + 1, :nz])
        message, slope_low_second_ref[here] = edge_terms(entering_second[here] + other_low_second_ref[here], column)
        totals[x][0] = totals[x][0] - message
    for x in range(ex):
        for y in range(ey):
            summed_ref[rows(x, y)] = totals[x][y].astype(BF16)

    node = node_ref[...].reshape(-1, features)
    update = dot(summed_ref[...], node_weight_ref[...])
    gate = sigmoid(update)
    new_ref[...] = (node.astype(F32) + update * gate).astype(BF16).reshape(new_ref.shape)
    cotangent = cotangent_ref[...].reshape(-1, features).astype(F32)
    update_ref[...] = (cotangent * (gate * (1.0 + update * (1.0 - gate)))).astype(BF16)
    grad_summed = dot_nt(update_ref[...], node_weight_ref[...]).astype(BF16)
    pair_target, extra = grad_pair_first_ref, 0
    if near_send_ref is not None:
        pair_target, extra = near_send_ref, near_send_ref.shape[0] - rows_first
    for y in range(ey):
        low, top = grad_summed[rows(0, y)], grad_summed[rows(ex - 1, y)]
        pair_target[extra + y * nz : extra + (y + 1) * nz] = jnp.where(even_first, top, low)
        grad_odd_first_ref[part(y)] = jnp.where(even_first, low, top)
    for x in range(ex):
        low, top = grad_summed[rows(x, 0)], grad_summed[rows(x, ey - 1)]
        grad_pair_second_ref[part(x)] = jnp.where(even_second, top, low)
        grad_odd_second_ref[part(x)] = jnp.where(even_second, low, top)
    wide = grad_summed.astype(F32)

    count = ex * ey * nz
    for index in range(ey + ex):
        cell = rows(0, index) if index < ey else rows(index - ey, 0)
        slope = slope_low_first_ref[part(index)] if index < ey else slope_low_second_ref[part(index - ey)]
        grad = -wide[cell] * slope
        grad_low_ref[part(index)] = grad
        grads_ref[3 * count + index * nz : 3 * count + (index + 1) * nz] = grad.astype(BF16)
    for x in range(ex):
        for y in range(ey):
            here = rows(x, y)
            mine = wide[here]
            lead = [
                mine - wide[rows(x + 1, y)] if x + 1 < ex else mine,
                mine - wide[rows(x, y + 1)] if y + 1 < ey else mine,
                mine - pltpu.roll(mine, nz - 1, 0),
            ]
            for direction in range(3):
                if direction == 0 and x == ex - 1:
                    slope = slope_top_first_ref[part(y)]
                elif direction == 1 and y == ey - 1:
                    slope = slope_top_second_ref[part(x)]
                else:
                    slope = slope_ref[direction, here]
                grad = lead[direction] * slope
                grad_ref[direction, here] = grad
                start = direction * count + (x * ey + y) * nz
                grads_ref[start : start + nz] = grad.astype(BF16)
    for x in range(ex):
        for y in range(ey):
            here = rows(x, y)
            third = grad_ref[2, here]
            own_ref[here] = grad_ref[0, here] + grad_ref[1, here] + third
            enter = pltpu.roll(third, 1, 0)
            enter = enter + (grad_ref[0, rows(x - 1, y)] if x > 0 else grad_low_ref[part(y)])
            enter = enter + (grad_ref[1, rows(x, y - 1)] if y > 0 else grad_low_ref[part(ey + x)])
            enter_ref[here] = enter

    grads_low = grads_ref[3 * count :]
    total_ref[:features] = dot_tn(
        jnp.concatenate([node, node_below_first, node_below_second], axis=0),
        jnp.concatenate([own_ref[...].astype(BF16), grads_low], axis=0),
    )
    tops = [grads_ref[((ex - 1) * ey + y) * nz : ((ex - 1) * ey + y + 1) * nz] for y in range(ey)]
    tops += [grads_ref[count + (x * ey + ey - 1) * nz : count + (x * ey + ey) * nz] for x in range(ex)]
    total_ref[features : 2 * features] = dot_tn(
        jnp.concatenate([node, node_above_first, node_above_second], axis=0),
        jnp.concatenate([enter_ref[...].astype(BF16), *tops], axis=0),
    )
    edges = edge_ref[...].reshape(-1, features)
    total_ref[2 * features : 3 * features] = dot_tn(
        jnp.concatenate([edges, edge_below_first, edge_below_second], axis=0), grads_ref[...]
    )
    total_ref[3 * features :] = dot_tn(summed_ref[...], update_ref[...])

    if near_send_ref is None:
        keep_ref[...] = total_ref[...]
        return
    planes = keep_ref.shape[0]
    seconds, chunk = lax.axis_size("gy"), keep_ref.shape[1] // lax.axis_size("gy")
    edge_rows, node_rows = chunk * 3 // 4, chunk // 4
    core, plane = at_first % 2, at_first // 2
    for block in range(planes):
        for second in range(seconds):
            there = (plane ^ block) * 2
            start = second * chunk
            for flip in (core, 1 - core):
                device = (there + flip) * seconds + (at_second ^ second)
                edge = total_ref[pl.ds(pl.multiple_of(device * edge_rows, 8), edge_rows)]
                node = total_ref[pl.ds(pl.multiple_of(3 * features + device * node_rows, 8), node_rows)]
                if flip is core:
                    keep_ref[block, start : start + edge_rows] = edge
                    keep_ref[block, start + edge_rows : start + chunk] = node
                else:
                    near = seconds // 2
                    if second < near:
                        send_ref, send_at = near_send_ref, (block * near + second) * chunk
                    else:
                        send_ref, send_at = far_send_ref, (block * (seconds - near) + second - near) * chunk
                    send_ref[send_at : send_at + edge_rows] = edge.astype(BF16)
                    send_ref[send_at + edge_rows : send_at + chunk] = node.astype(BF16)


def node_grad_kernel(
    dims, own_ref, enter_ref, slope_top_first_ref, slope_low_first_ref, slope_top_second_ref, slope_low_second_ref,
    pair_first_ref, odd_first_ref, pair_second_ref, odd_second_ref, cotangent_ref, weight_ref, out_ref,
):
    ex, ey, nz, features = dims
    even_first, even_second = is_even("gx"), is_even("gy")
    extra = pair_first_ref.shape[0] - ey * nz

    def rows(x, y):
        return slice((x * ey + y) * nz, (x * ey + y + 1) * nz)

    def part(index):
        return slice(index * nz, (index + 1) * nz)

    own, enter = [], []
    for x in range(ex):
        for y in range(ey):
            grad = own_ref[rows(x, y)]
            pair_first = pair_first_ref[extra + y * nz : extra + (y + 1) * nz].astype(F32)
            odd_first = odd_first_ref[part(y)].astype(F32)
            pair_second, odd_second = pair_second_ref[part(x)].astype(F32), odd_second_ref[part(x)].astype(F32)
            if x == ex - 1:
                grad = grad - jnp.where(even_first, pair_first, odd_first) * slope_top_first_ref[part(y)]
            if y == ey - 1:
                grad = grad - jnp.where(even_second, pair_second, odd_second) * slope_top_second_ref[part(x)]
            own.append(grad.astype(BF16))
            grad = enter_ref[rows(x, y)]
            if x == 0:
                grad = grad + jnp.where(even_first, odd_first, pair_first) * slope_low_first_ref[part(y)]
            if y == 0:
                grad = grad + jnp.where(even_second, odd_second, pair_second) * slope_low_second_ref[part(x)]
            enter.append(grad.astype(BF16))
    result = dot_nt(jnp.concatenate(own, axis=0), weight_ref[:features])
    result = result + dot_nt(jnp.concatenate(enter, axis=0), weight_ref[features : 2 * features])
    result = result + cotangent_ref[...].reshape(-1, features).astype(F32)
    out_ref[...] = result.astype(BF16).reshape(out_ref.shape)


def pair_sum_kernel(first, keep_ref, received_ref, kept_ref, *send_refs):
    size = kept_ref.shape[0]
    for plane in range(len(send_refs) + 1):
        total = keep_ref[plane, first : first + size] + received_ref[plane * size : (plane + 1) * size].astype(F32)
        if plane == 0:
            kept_ref[...] = total
        else:
            send_refs[plane - 1][...] = total.astype(BF16)


def plane_sum_kernel(received, *refs):
    kept_ref, arrived, outs = refs[0], refs[1 : received + 1], refs[received + 1 :]
    chunk = outs[0].shape[0]
    for index, out in enumerate(outs):
        here = slice(index * chunk, (index + 1) * chunk)
        total = kept_ref[here]
        for ref in arrived:
            total = total + ref[here].astype(F32)
        out[...] = total.astype(out.dtype)


def last_sum_kernel(keep_ref, *refs):
    received, edge_ref, node_ref = refs[:-2], refs[-2], refs[-1]
    total = keep_ref[...]
    for ref in received:
        total = total + ref[...].astype(F32)
    lanes = edge_ref.shape[1]
    pieces = total.shape[1] // lanes
    edge_rows, node_rows = edge_ref.shape[0] // pieces, node_ref.shape[0] // pieces
    for piece in range(pieces):
        across = slice(piece * lanes, (piece + 1) * lanes)
        edge_ref[pl.ds(piece, edge_rows, stride=pieces)] = total[:edge_rows, across]
        node_ref[pl.ds(piece, node_rows, stride=pieces)] = total[edge_rows:, across]


def local(node_features, edge_features, open_faces, edge_weight, node_weight, cotangent):
    dims = ex, ey, nz, features = node_features.shape
    firsts, seconds = lax.axis_size("gx"), lax.axis_size("gy")
    devices = firsts * seconds
    count = ex * ey * nz

    face_first, face_second = (ey * nz, features), (ex * nz, features)
    packed_first, packed_second = (2 * ey * nz + PAD, features), (2 * ex * nz + PAD, features)
    copies = 3 * (ex + ey) + 1
    pair_first, odd_first, pair_second, odd_second = call(
        functools.partial(pack_kernel, dims),
        [(packed_first, BF16)] * 2 + [(packed_second, BF16)] * 2,
        [node_features, edge_features, open_faces],
        scratch=[pltpu.VMEM(open_faces.shape, jnp.int32), pltpu.SemaphoreType.DMA((copies,))],
        far=3,
    )
    pair_second = swapped(pair_second, "gy", 0)
    odd_second = swapped(odd_second, "gy", 1)
    odd_first = swapped(odd_first, "gx", 1)
    pair_first = swapped(pair_first, "gx", 0)
    before = [((count, features), F32), ((3, count, features), F32)] + [(face_first, F32)] * 2 + [(face_second, F32)] * 2
    before = call(
        functools.partial(before_kernel, dims),
        before,
        [node_features, edge_features, edge_weight, open_faces],
        scratch=[
            pltpu.VMEM((count, features), F32),
            pltpu.VMEM((3, count, features), F32),
            pltpu.VMEM((3, count, features), F32),
            pltpu.VMEM(node_features.shape, BF16),
            pltpu.VMEM(edge_features.shape, BF16),
            pltpu.VMEM(edge_weight.shape, BF16),
            pltpu.VMEM(open_faces.shape, jnp.int32),
            pltpu.SemaphoreType.DMA((4,)),
        ],
        limit=12 << 20,
        far=4,
    )
    total_rows = 4 * features
    chunk = total_rows // devices
    by_hand = (
        total_rows % devices == 0
        and chunk % 64 == 0
        and features % 128 == 0
        and firsts % 2 == 0
        and firsts & (firsts - 1) == 0
        and seconds & (seconds - 1) == 0
        and seconds > 1
    )
    planes = firsts // 2
    outs = [(node_features.shape, BF16), (face_first, BF16), (face_second, BF16), (face_second, BF16)]
    outs += [((count, features), F32)] * 2 + [(face_first, F32)] * 2 + [(face_second, F32)] * 2
    if by_hand:
        near, far = seconds // 2 * chunk, (seconds - seconds // 2) * chunk
        outs += [((planes * far, features), BF16), ((planes * near + ey * nz, features), BF16)]
        outs += [((planes, near + far, features), F32)]

        def kernel(*refs):
            layer_kernel(dims, *refs[:26], None, *refs[26:])

    else:
        outs += [(face_first, BF16), ((total_rows, features), F32)]

        def kernel(*refs):
            layer_kernel(dims, *refs[:27], None, None, *refs[27:])

    low_rows = (ex + ey) * nz
    results = call(
        kernel,
        outs,
        [
            *before, edge_weight, node_weight, node_features, edge_features, open_faces, cotangent,
            pair_first, odd_first, pair_second, odd_second,
        ],
        scratch=[
            pltpu.VMEM((count, features), BF16),
            pltpu.VMEM((count, features), BF16),
            pltpu.VMEM((3, count, features), F32),
            pltpu.VMEM((low_rows, features), F32),
            pltpu.VMEM((3 * count + low_rows, features), BF16),
            pltpu.VMEM((total_rows, features), F32),
        ],
        limit=14 << 20,
    )
    new_nodes, odd_first, pair_second, odd_second = results[:4]
    keep = results[-1]
    if by_hand:
        far_received = swapped(results[10], "gx", 0)
    received = swapped(results[-2], "gx", 0)
    pair_second = swapped(pair_second, "gy", 0)
    odd_second = swapped(odd_second, "gy", 1)
    odd_first = swapped(odd_first, "gx", 1)
    (node_grad,) = call(
        functools.partial(node_grad_kernel, dims),
        [(node_features.shape, BF16)],
        [
            *results[4:10], received, odd_first, pair_second, odd_second, cotangent, edge_weight,
        ],
    )
    if not by_hand:
        total = keep
        edge_part = lax.psum_scatter(total[: 3 * features].reshape(-1), ("gx", "gy"), scatter_dimension=0, tiled=True)
        node_part = lax.psum_scatter(total[3 * features :].reshape(-1), ("gx", "gy"), scatter_dimension=0, tiled=True)
        return new_nodes, node_grad, edge_part, node_part

    def summed_pairs(first, size, arrived):
        return call(
            functools.partial(pair_sum_kernel, first),
            [((size, features), F32)] + [((size, features), BF16)] * (planes - 1),
            [keep, arrived],
        )

    far_kept, *far_sends = summed_pairs(near, far, far_received)
    near_kept, *near_sends = summed_pairs(0, near, received)

    def over_planes(values):
        arrived = []
        for index, value in enumerate(values):
            arrived.append(exchanged(value, "gx", 2 * (index + 1)))
        return arrived

    far_arrived, near_arrived = over_planes(far_sends), over_planes(near_sends)
    piece = ((chunk, features), BF16)
    far_sends = call(
        functools.partial(plane_sum_kernel, planes - 1), [piece] * (seconds - seconds // 2), [far_kept, *far_arrived]
    )
    kept, *near_sends = call(
        functools.partial(plane_sum_kernel, planes - 1),
        [((chunk, features), F32)] + [piece] * (seconds // 2 - 1),
        [near_kept, *near_arrived],
    )
    arrived = []
    for index, value in enumerate([*near_sends, *far_sends]):
        arrived.append(exchanged(value, "gy", index + 1))
    pieces = features // 128
    edge_part, node_part = call(
        last_sum_kernel, [((chunk * 3 // 4 * pieces, 128), F32), ((chunk // 4 * pieces, 128), F32)], [kept, *arrived]
    )
    return new_nodes, node_grad, edge_part.reshape(-1), node_part.reshape(-1)


def solution(mesh):
    placed = (
        P("gx", "gy", None, None),
        P(None, "gx", "gy", None, None),
        P(None, "gx", "gy", None),
        P(),
        P(),
        P("gx", "gy", None, None),
    )
    return jax.shard_map(
        local,
        mesh=mesh,
        in_specs=placed,
        out_specs=(
            P("gx", "gy", None, None),
            P("gx", "gy", None, None),
            P(("gx", "gy")),
            P(("gx", "gy")),
        ),
        check_vma=False,
    )
```

```python
import functools

import jax
import jax.numpy as jnp
from jax import lax
from jax.experimental import pallas as pl
from jax.experimental.pallas import tpu as pltpu
from jax.sharding import PartitionSpec as P

F32 = jnp.float32
BF16 = jnp.bfloat16
PAD = 16


def swapped(value, axis, first):
    count = lax.axis_size(axis)
    lower = range(first, count - 1, 2)
    return lax.ppermute(value, axis, [(at, at + 1) for at in lower] + [(at + 1, at) for at in lower])


def exchanged(value, axis, flip):
    count = lax.axis_size(axis)
    return lax.ppermute(value, axis, [(source, source ^ flip) for source in range(count)])


def dot(left, right):
    return jnp.dot(left, right, preferred_element_type=F32)


def dot_nt(left, right):
    return lax.dot_general(left, right, (((1,), (1,)), ((), ())), preferred_element_type=F32)


def dot_tn(left, right):
    return lax.dot_general(left, right, (((0,), (0,)), ((), ())), preferred_element_type=F32)


def column_of(row):
    size = row.shape[-1]
    spread = jnp.broadcast_to(row, (size, size))
    down = lax.broadcasted_iota(jnp.int32, (size, size), 0)
    across = lax.broadcasted_iota(jnp.int32, (size, size), 1)
    return jnp.sum(jnp.where(down == across, spread, 0.0), axis=1, keepdims=True)


def sigmoid(values):
    return 0.5 * jnp.tanh(0.5 * values) + 0.5


def call(kernel, outs, args, scratch=(), limit=4 << 20, cost=None, far=0):
    args = [pltpu.with_memory_space_constraint(arg, pltpu.HBM) for arg in args[:far]] + list(args[far:])
    return pl.pallas_call(
        kernel,
        out_shape=[jax.ShapeDtypeStruct(shape, dtype) for shape, dtype in outs],
        in_specs=[pl.BlockSpec(memory_space=pltpu.HBM)] * far + [pl.BlockSpec(memory_space=pltpu.VMEM)] * (len(args) - far),
        out_specs=[pl.BlockSpec(memory_space=pltpu.VMEM)] * len(outs),
        scratch_shapes=list(scratch),
        compiler_params=pltpu.CompilerParams(vmem_limit_bytes=limit),
        cost_estimate=cost,
    )(*args)


def spread_rows(rows, count):
    down = lax.broadcasted_iota(jnp.int32, (count, rows[0].shape[-1]), 0)
    tile = jnp.zeros((count, rows[0].shape[-1]), F32)
    for index, row in enumerate(rows):
        tile = jnp.where(down == index, row, tile)
    return tile


def is_even(axis):
    return lax.axis_index(axis) % 2 == 0


def pack_kernel(
    dims, node_ref, edge_ref, faces_ref, pair_first_ref, odd_first_ref, pair_second_ref, odd_second_ref, open_ref, sems
):
    ex, ey, nz, _ = dims
    faces_copy = pltpu.make_async_copy(faces_ref, open_ref, sems.at[0])
    faces_copy.start()

    def upward(ref, direction, cells):
        pairs = []
        for index, (x, y) in enumerate(cells):
            pairs.append((node_ref.at[x, y], ref.at[pl.ds(index * nz, nz)]))
            pairs.append((edge_ref.at[direction, x, y], ref.at[pl.ds((len(cells) + index) * nz, nz)]))
        return pairs

    def downward(ref, cells):
        return [(node_ref.at[x, y], ref.at[pl.ds(index * nz, nz)]) for index, (x, y) in enumerate(cells)]

    plans, used = [], 1
    for direction, axis, pair_ref, odd_ref, top, low in (
        (1, "gy", pair_second_ref, odd_second_ref, [(x, ey - 1) for x in range(ex)], [(x, 0) for x in range(ex)]),
        (0, "gx", pair_first_ref, odd_first_ref, [(ex - 1, y) for y in range(ey)], [(0, y) for y in range(ey)]),
    ):
        choices = [upward(up, direction, top) + downward(down, low) for up, down in ((pair_ref, odd_ref), (odd_ref, pair_ref))]
        copies = [
            [pltpu.make_async_copy(source, target, sems.at[used + index]) for index, (source, target) in enumerate(pairs)]
            for pairs in choices
        ]
        used += len(copies[0])
        plans.append((is_even(axis), copies, (pair_ref, odd_ref), 2 * len(top) * nz, (direction, top)))
    for even, copies, _, _, _ in plans:
        for wanted, group in ((even, copies[0]), (jnp.logical_not(even), copies[1])):
            @pl.when(wanted)
            def _():
                for copy in group:
                    copy.start()
    faces_copy.wait()
    for even, copies, refs, start, (direction, top) in plans:
        mask = spread_rows([open_ref[direction, x, y : y + 1].astype(F32) for x, y in top], PAD).astype(BF16)
        for ref in refs:
            ref[start:, :nz] = mask
        for wanted, group in ((even, copies[0]), (jnp.logical_not(even), copies[1])):
            @pl.when(wanted)
            def _():
                for copy in group:
                    copy.wait()


def edge_terms(preact, open_column):
    gate = sigmoid(preact)
    opened = gate * open_column
    message = (preact * opened).astype(BF16).astype(F32)
    return message, opened * (1.0 + preact * (1.0 - gate))


def halves(even, pair_ref, odd_ref, rows):
    def pick(first, second, start, stop):
        return jnp.where(even, first[start:stop], second[start:stop])

    return (
        pick(pair_ref, odd_ref, 0, rows),
        pick(odd_ref, pair_ref, 0, rows),
        pick(odd_ref, pair_ref, rows, 2 * rows),
        pick(odd_ref, pair_ref, 2 * rows, 2 * rows + PAD).astype(F32),
    )


def before_kernel(
    dims, node_ref, edge_ref, weight_ref, faces_ref,
    sum_ref, slope_ref, stored_top_first_ref, other_low_first_ref, stored_top_second_ref, other_low_second_ref,
    other_ref, stored_ref, message_ref, node_here, edge_here, weight_here, open_ref, sems,
):
    ex, ey, nz, features = dims
    copies = [
        pltpu.make_async_copy(node_ref, node_here, sems.at[0]),
        pltpu.make_async_copy(weight_ref, weight_here, sems.at[1]),
        pltpu.make_async_copy(edge_ref, edge_here, sems.at[2]),
        pltpu.make_async_copy(faces_ref, open_ref, sems.at[3]),
    ]
    for copy in copies:
        copy.start()

    def rows(x, y):
        return slice((x * ey + y) * nz, (x * ey + y + 1) * nz)

    def part(index):
        return slice(index * nz, (index + 1) * nz)

    copies[0].wait()
    copies[1].wait()
    node = node_here[...].reshape(-1, features)
    own = dot(node, weight_here[:features])
    other_ref[...] = dot(node, weight_here[features : 2 * features])
    copies[2].wait()
    copies[3].wait()
    for direction in range(3):
        stored_ref[direction] = own + dot(edge_here[direction].reshape(-1, features), weight_here[2 * features :])
    inside_third = jnp.where(lax.broadcasted_iota(jnp.int32, (nz, 1), 0) < nz - 1, 1.0, 0.0)
    for y in range(ey):
        stored_top_first_ref[part(y)] = stored_ref[0, rows(ex - 1, y)]
        other_low_first_ref[part(y)] = other_ref[rows(0, y)]
    for x in range(ex):
        stored_top_second_ref[part(x)] = stored_ref[1, rows(x, ey - 1)]
        other_low_second_ref[part(x)] = other_ref[rows(x, 0)]
        for y in range(ey):
            here = rows(x, y)
            column = [column_of(open_ref[direction, x, y : y + 1].astype(F32)) for direction in range(3)]
            if x + 1 < ex:
                beyond = other_ref[rows(x + 1, y)]
                message_ref[0, here], slope_ref[0, here] = edge_terms(stored_ref[0, here] + beyond, column[0])
            if y + 1 < ey:
                beyond = other_ref[rows(x, y + 1)]
                message_ref[1, here], slope_ref[1, here] = edge_terms(stored_ref[1, here] + beyond, column[1])
            beyond = pltpu.roll(other_ref[here], nz - 1, 0)
            message_ref[2, here], slope_ref[2, here] = edge_terms(stored_ref[2, here] + beyond, column[2] * inside_third)
    for x in range(ex):
        for y in range(ey):
            here = rows(x, y)
            third = message_ref[2, here]
            total = third - pltpu.roll(third, 1, 0)
            if x + 1 < ex:
                total = total + message_ref[0, here]
            if x > 0:
                total = total - message_ref[0, rows(x - 1, y)]
            if y + 1 < ey:
                total = total + message_ref[1, here]
            if y > 0:
                total = total - message_ref[1, rows(x, y - 1)]
            sum_ref[here] = total


def layer_kernel(
    dims,
    sum_ref, slope_ref, stored_top_first_ref, other_low_first_ref, stored_top_second_ref, other_low_second_ref,
    weight_ref, node_weight_ref, node_ref, edge_ref, open_ref, cotangent_ref,
    pair_first_ref, odd_first_ref, pair_second_ref, odd_second_ref,
    new_ref, grad_odd_first_ref, grad_pair_second_ref, grad_odd_second_ref,
    own_ref, enter_ref, slope_top_first_ref, slope_low_first_ref, slope_top_second_ref, slope_low_second_ref,
    grad_pair_first_ref, far_send_ref, total_ref,
    summed_ref, update_ref, grad_ref, grad_low_ref, grads_ref,
):
    ex, ey, nz, features = dims
    at_first, at_second = lax.axis_index("gx"), lax.axis_index("gy")
    inside_first = (at_first < lax.axis_size("gx") - 1).astype(F32)
    inside_second = (at_second < lax.axis_size("gy") - 1).astype(F32)
    even_first, even_second = is_even("gx"), is_even("gy")

    def rows(x, y):
        return slice((x * ey + y) * nz, (x * ey + y + 1) * nz)

    def part(index):
        return slice(index * nz, (index + 1) * nz)

    rows_first, rows_second = ey * nz, ex * nz
    node_above_first, node_below_first, edge_below_first, mask_first = halves(
        even_first, pair_first_ref, odd_first_ref, rows_first
    )
    node_above_second, node_below_second, edge_below_second, mask_second = halves(
        even_second, pair_second_ref, odd_second_ref, rows_second
    )
    other_weight = weight_ref[features : 2 * features]
    above_first, above_second = dot(node_above_first, other_weight), dot(node_above_second, other_weight)
    entering_first = dot(node_below_first, weight_ref[:features]) + dot(edge_below_first, weight_ref[2 * features :])
    entering_second = dot(node_below_second, weight_ref[:features]) + dot(edge_below_second, weight_ref[2 * features :])
    totals = [[sum_ref[rows(x, y)] for y in range(ey)] for x in range(ex)]
    for y in range(ey):
        here = part(y)
        column = column_of(open_ref[0, ex - 1, y : y + 1].astype(F32)) * inside_first
        message, slope_top_first_ref[here] = edge_terms(stored_top_first_ref[here] + above_first[here], column)
        totals[ex - 1][y] = totals[ex - 1][y] + message
        column = column_of(mask_first[y : y + 1, :nz])
        message, slope_low_first_ref[here] = edge_terms(entering_first[here] + other_low_first_ref[here], column)
        totals[0][y] = totals[0][y] - message
    for x in range(ex):
        here = part(x)
        column = column_of(open_ref[1, x, ey - 1 : ey].astype(F32)) * inside_second
        message, slope_top_second_ref[here] = edge_terms(stored_top_second_ref[here] + above_second[here], column)
        totals[x][ey - 1] = totals[x][ey - 1] + message
        column = column_of(mask_second[x : x + 1, :nz])
        message, slope_low_second_ref[here] = edge_terms(entering_second[here] + other_low_second_ref[here], column)
        totals[x][0] = totals[x][0] - message
    for x in range(ex):
        for y in range(ey):
            summed_ref[rows(x, y)] = totals[x][y].astype(BF16)

    node = node_ref[...].reshape(-1, features)
    update = dot(summed_ref[...], node_weight_ref[...])
    gate = sigmoid(update)
    new_ref[...] = (node.astype(F32) + update * gate).astype(BF16).reshape(new_ref.shape)
    cotangent = cotangent_ref[...].reshape(-1, features).astype(F32)
    update_ref[...] = (cotangent * (gate * (1.0 + update * (1.0 - gate)))).astype(BF16)
    grad_summed = dot_nt(update_ref[...], node_weight_ref[...]).astype(BF16)
    for y in range(ey):
        low, top = grad_summed[rows(0, y)], grad_summed[rows(ex - 1, y)]
        grad_pair_first_ref[part(y)] = jnp.where(even_first, top, low)
        grad_odd_first_ref[part(y)] = jnp.where(even_first, low, top)
    for x in range(ex):
        low, top = grad_summed[rows(x, 0)], grad_summed[rows(x, ey - 1)]
        grad_pair_second_ref[part(x)] = jnp.where(even_second, top, low)
        grad_odd_second_ref[part(x)] = jnp.where(even_second, low, top)
    wide = grad_summed.astype(F32)

    count = ex * ey * nz
    for index in range(ey + ex):
        cell = rows(0, index) if index < ey else rows(index - ey, 0)
        slope = slope_low_first_ref[part(index)] if index < ey else slope_low_second_ref[part(index - ey)]
        grad = -wide[cell] * slope
        grad_low_ref[part(index)] = grad
        grads_ref[3 * count + index * nz : 3 * count + (index + 1) * nz] = grad.astype(BF16)
    for x in range(ex):
        for y in range(ey):
            here = rows(x, y)
            mine = wide[here]
            lead = [
                mine - wide[rows(x + 1, y)] if x + 1 < ex else mine,
                mine - wide[rows(x, y + 1)] if y + 1 < ey else mine,
                mine - pltpu.roll(mine, nz - 1, 0),
            ]
            for direction in range(3):
                if direction == 0 and x == ex - 1:
                    slope = slope_top_first_ref[part(y)]
                elif direction == 1 and y == ey - 1:
                    slope = slope_top_second_ref[part(x)]
                else:
                    slope = slope_ref[direction, here]
                grad = lead[direction] * slope
                grad_ref[direction, here] = grad
                start = direction * count + (x * ey + y) * nz
                grads_ref[start : start + nz] = grad.astype(BF16)
    for x in range(ex):
        for y in range(ey):
            here = rows(x, y)
            third = grad_ref[2, here]
            own_ref[here] = grad_ref[0, here] + grad_ref[1, here] + third
            enter = pltpu.roll(third, 1, 0)
            enter = enter + (grad_ref[0, rows(x - 1, y)] if x > 0 else grad_low_ref[part(y)])
            enter = enter + (grad_ref[1, rows(x, y - 1)] if y > 0 else grad_low_ref[part(ey + x)])
            enter_ref[here] = enter

    grads_low = grads_ref[3 * count :]
    total_ref[:features] = dot_tn(
        jnp.concatenate([node, node_below_first, node_below_second], axis=0),
        jnp.concatenate([own_ref[...].astype(BF16), grads_low], axis=0),
    )
    tops = [grads_ref[((ex - 1) * ey + y) * nz : ((ex - 1) * ey + y + 1) * nz] for y in range(ey)]
    tops += [grads_ref[count + (x * ey + ey - 1) * nz : count + (x * ey + ey) * nz] for x in range(ex)]
    total_ref[features : 2 * features] = dot_tn(
        jnp.concatenate([node, node_above_first, node_above_second], axis=0),
        jnp.concatenate([enter_ref[...].astype(BF16), *tops], axis=0),
    )
    edges = edge_ref[...].reshape(-1, features)
    total_ref[2 * features : 3 * features] = dot_tn(
        jnp.concatenate([edges, edge_below_first, edge_below_second], axis=0), grads_ref[...]
    )
    total_ref[3 * features :] = dot_tn(summed_ref[...], update_ref[...])

    if far_send_ref is not None:
        seconds = lax.axis_size("gy")
        send_chunks(total_ref, far_send_ref, range(seconds // 2, seconds))


def chunk_of(total_ref, flip, plane, second):
    devices = lax.axis_size("gx") * lax.axis_size("gy")
    node_rows = total_ref.shape[0] // 4 // devices
    edge_rows = 3 * node_rows
    at_first, at_second = lax.axis_index("gx"), lax.axis_index("gy")
    first = ((at_first // 2) ^ plane) * 2 + (1 - at_first % 2 if flip else at_first % 2)
    device = first * lax.axis_size("gy") + (at_second ^ second)
    edge_at = pl.multiple_of(device * edge_rows, PAD)
    node_at = pl.multiple_of(total_ref.shape[0] * 3 // 4 + device * node_rows, PAD)
    return (edge_at, edge_rows), (node_at, node_rows)


def send_chunks(total_ref, send_ref, seconds):
    at = 0
    for plane in range(lax.axis_size("gx") // 2):
        for second in seconds:
            for start, size in chunk_of(total_ref, True, plane, second):
                send_ref[at : at + size] = total_ref[pl.ds(start, size)].astype(BF16)
                at += size


def near_pack_kernel(total_ref, grad_ref, send_ref):
    send_chunks(total_ref, send_ref, range(lax.axis_size("gy") // 2))
    send_ref[send_ref.shape[0] - grad_ref.shape[0] :] = grad_ref[...]


def node_grad_kernel(
    dims, own_ref, enter_ref, slope_top_first_ref, slope_low_first_ref, slope_top_second_ref, slope_low_second_ref,
    pair_first_ref, odd_first_ref, pair_second_ref, odd_second_ref, cotangent_ref, weight_ref, out_ref,
):
    ex, ey, nz, features = dims
    even_first, even_second = is_even("gx"), is_even("gy")
    extra = pair_first_ref.shape[0] - ey * nz

    def rows(x, y):
        return slice((x * ey + y) * nz, (x * ey + y + 1) * nz)

    def part(index):
        return slice(index * nz, (index + 1) * nz)

    own, enter = [], []
    for x in range(ex):
        for y in range(ey):
            grad = own_ref[rows(x, y)]
            pair_first = pair_first_ref[extra + y * nz : extra + (y + 1) * nz].astype(F32)
            odd_first = odd_first_ref[part(y)].astype(F32)
            pair_second, odd_second = pair_second_ref[part(x)].astype(F32), odd_second_ref[part(x)].astype(F32)
            if x == ex - 1:
                grad = grad - jnp.where(even_first, pair_first, odd_first) * slope_top_first_ref[part(y)]
            if y == ey - 1:
                grad = grad - jnp.where(even_second, pair_second, odd_second) * slope_top_second_ref[part(x)]
            own.append(grad.astype(BF16))
            grad = enter_ref[rows(x, y)]
            if x == 0:
                grad = grad + jnp.where(even_first, odd_first, pair_first) * slope_low_first_ref[part(y)]
            if y == 0:
                grad = grad + jnp.where(even_second, odd_second, pair_second) * slope_low_second_ref[part(x)]
            enter.append(grad.astype(BF16))
    result = dot_nt(jnp.concatenate(own, axis=0), weight_ref[:features])
    result = result + dot_nt(jnp.concatenate(enter, axis=0), weight_ref[features : 2 * features])
    result = result + cotangent_ref[...].reshape(-1, features).astype(F32)
    out_ref[...] = result.astype(BF16).reshape(out_ref.shape)


def pair_sum_kernel(seconds, total_ref, received_ref, kept_ref, *send_refs):
    at = 0
    for plane, out in enumerate((kept_ref, *send_refs)):
        here = 0
        for second in seconds:
            for start, size in chunk_of(total_ref, False, plane, second):
                total = total_ref[pl.ds(start, size)] + received_ref[at : at + size].astype(F32)
                out[here : here + size] = total.astype(out.dtype)
                at, here = at + size, here + size


def plane_sum_kernel(received, *refs):
    kept_ref, arrived, outs = refs[0], refs[1 : received + 1], refs[received + 1 :]
    chunk = outs[0].shape[0]
    for index, out in enumerate(outs):
        here = slice(index * chunk, (index + 1) * chunk)
        total = kept_ref[here]
        for ref in arrived:
            total = total + ref[here].astype(F32)
        out[...] = total.astype(out.dtype)


def last_sum_kernel(keep_ref, *refs):
    received, edge_ref, node_ref = refs[:-2], refs[-2], refs[-1]
    total = keep_ref[...]
    for ref in received:
        total = total + ref[...].astype(F32)
    lanes = edge_ref.shape[1]
    pieces = total.shape[1] // lanes
    edge_rows, node_rows = edge_ref.shape[0] // pieces, node_ref.shape[0] // pieces
    for piece in range(pieces):
        across = slice(piece * lanes, (piece + 1) * lanes)
        edge_ref[pl.ds(piece, edge_rows, stride=pieces)] = total[:edge_rows, across]
        node_ref[pl.ds(piece, node_rows, stride=pieces)] = total[edge_rows:, across]


def local(node_features, edge_features, open_faces, edge_weight, node_weight, cotangent):
    dims = ex, ey, nz, features = node_features.shape
    firsts, seconds = lax.axis_size("gx"), lax.axis_size("gy")
    devices = firsts * seconds
    count = ex * ey * nz

    face_first, face_second = (ey * nz, features), (ex * nz, features)
    packed_first, packed_second = (2 * ey * nz + PAD, features), (2 * ex * nz + PAD, features)
    copies = 3 * (ex + ey) + 1
    pair_first, odd_first, pair_second, odd_second = call(
        functools.partial(pack_kernel, dims),
        [(packed_first, BF16)] * 2 + [(packed_second, BF16)] * 2,
        [node_features, edge_features, open_faces],
        scratch=[pltpu.VMEM(open_faces.shape, jnp.int32), pltpu.SemaphoreType.DMA((copies,))],
        far=3,
    )
    pair_second = swapped(pair_second, "gy", 0)
    odd_second = swapped(odd_second, "gy", 1)
    odd_first = swapped(odd_first, "gx", 1)
    pair_first = swapped(pair_first, "gx", 0)
    before = [((count, features), F32), ((3, count, features), F32)] + [(face_first, F32)] * 2 + [(face_second, F32)] * 2
    before = call(
        functools.partial(before_kernel, dims),
        before,
        [node_features, edge_features, edge_weight, open_faces],
        scratch=[
            pltpu.VMEM((count, features), F32),
            pltpu.VMEM((3, count, features), F32),
            pltpu.VMEM((3, count, features), F32),
            pltpu.VMEM(node_features.shape, BF16),
            pltpu.VMEM(edge_features.shape, BF16),
            pltpu.VMEM(edge_weight.shape, BF16),
            pltpu.VMEM(open_faces.shape, jnp.int32),
            pltpu.SemaphoreType.DMA((4,)),
        ],
        limit=12 << 20,
        far=4,
    )
    total_rows = 4 * features
    chunk = total_rows // devices
    by_hand = (
        total_rows % devices == 0
        and chunk % 64 == 0
        and features % 128 == 0
        and firsts % 2 == 0
        and firsts & (firsts - 1) == 0
        and seconds & (seconds - 1) == 0
        and seconds > 1
    )
    planes = firsts // 2
    outs = [(node_features.shape, BF16), (face_first, BF16), (face_second, BF16), (face_second, BF16)]
    outs += [((count, features), F32)] * 2 + [(face_first, F32)] * 2 + [(face_second, F32)] * 2
    outs += [(face_first, BF16)]
    total_out = ((total_rows, features), F32)
    near, far = seconds // 2 * chunk, (seconds - seconds // 2) * chunk
    if by_hand:
        outs += [((planes * far, features), BF16), total_out]
        kernel = functools.partial(layer_kernel, dims)
    else:
        outs += [total_out]

        def kernel(*refs):
            layer_kernel(dims, *refs[:27], None, *refs[27:])

    low_rows = (ex + ey) * nz
    results = call(
        kernel,
        outs,
        [
            *before, edge_weight, node_weight, node_features, edge_features, open_faces, cotangent,
            pair_first, odd_first, pair_second, odd_second,
        ],
        scratch=[
            pltpu.VMEM((count, features), BF16),
            pltpu.VMEM((count, features), BF16),
            pltpu.VMEM((3, count, features), F32),
            pltpu.VMEM((low_rows, features), F32),
            pltpu.VMEM((3 * count + low_rows, features), BF16),
        ],
        limit=14 << 20,
    )
    new_nodes, odd_first, pair_second, odd_second = results[:4]
    received, total = results[10], results[-1]
    if by_hand:
        far_received = swapped(results[11], "gx", 0)
        (received,) = call(near_pack_kernel, [((planes * near + ey * nz, features), BF16)], [total, received])
    received = swapped(received, "gx", 0)
    pair_second = swapped(pair_second, "gy", 0)
    odd_second = swapped(odd_second, "gy", 1)
    odd_first = swapped(odd_first, "gx", 1)
    (node_grad,) = call(
        functools.partial(node_grad_kernel, dims),
        [(node_features.shape, BF16)],
        [
            *results[4:10], received, odd_first, pair_second, odd_second, cotangent, edge_weight,
        ],
    )
    if not by_hand:
        edge_part = lax.psum_scatter(total[: 3 * features].reshape(-1), ("gx", "gy"), scatter_dimension=0, tiled=True)
        node_part = lax.psum_scatter(total[3 * features :].reshape(-1), ("gx", "gy"), scatter_dimension=0, tiled=True)
        return new_nodes, node_grad, edge_part, node_part

    def summed_pairs(places, size, arrived):
        return call(
            functools.partial(pair_sum_kernel, places),
            [((size, features), F32)] + [((size, features), BF16)] * (planes - 1),
            [total, arrived],
        )

    far_kept, *far_sends = summed_pairs(range(seconds // 2, seconds), far, far_received)
    near_kept, *near_sends = summed_pairs(range(seconds // 2), near, received)

    def over_planes(values):
        arrived = []
        for index, value in enumerate(values):
            arrived.append(exchanged(value, "gx", 2 * (index + 1)))
        return arrived

    far_arrived, near_arrived = over_planes(far_sends), over_planes(near_sends)
    piece = ((chunk, features), BF16)
    far_sends = call(
        functools.partial(plane_sum_kernel, planes - 1), [piece] * (seconds - seconds // 2), [far_kept, *far_arrived]
    )
    kept, *near_sends = call(
        functools.partial(plane_sum_kernel, planes - 1),
        [((chunk, features), F32)] + [piece] * (seconds // 2 - 1),
        [near_kept, *near_arrived],
    )
    arrived = []
    for index, value in enumerate([*near_sends, *far_sends]):
        arrived.append(exchanged(value, "gy", index + 1))
    pieces = features // 128
    edge_part, node_part = call(
        last_sum_kernel, [((chunk * 3 // 4 * pieces, 128), F32), ((chunk // 4 * pieces, 128), F32)], [kept, *arrived]
    )
    return new_nodes, node_grad, edge_part.reshape(-1), node_part.reshape(-1)


def solution(mesh):
    placed = (
        P("gx", "gy", None, None),
        P(None, "gx", "gy", None, None),
        P(None, "gx", "gy", None),
        P(),
        P(),
        P("gx", "gy", None, None),
    )
    return jax.shard_map(
        local,
        mesh=mesh,
        in_specs=placed,
        out_specs=(
            P("gx", "gy", None, None),
            P("gx", "gy", None, None),
            P(("gx", "gy")),
            P(("gx", "gy")),
        ),
        check_vma=False,
    )
```
